256 devices in a mesh: samples: 64 (over z, y, core), groups: 4 (over x).
Axes of the slice: x: 4, y: 4, z: 8, core: 2. Of those that a mesh axis runs over, the one named last changes fastest.
Arguments:
- observed: bfloat16 [1024, 81920], P('samples', 'groups'), may hold values from -200 to 200
- labels: int32 [81920], P('groups'), may hold values from 0 to 255, as said below
- comp_sizes: int32 [256], P('groups'), may hold values from 128 to 512, as said below
Outputs:
- whitened: bfloat16 [1024, 81920], P('samples', 'groups')
The draws below stay inside these ranges and needn't reach their ends.
Inputs may be any that keep to these rules, and one draw needn't show every extreme that they name: Group g's columns (g * 20480 to (g + 1) * 20480 - 1) carry exactly the labels g * 64 to (g + 1) * 64 - 1, and label c stands on exactly comp_sizes[c] columns. `comp_sizes`: in every group one component has exactly 512 variables; components 2k and 2k + 1 (k = 0, 1, ...) together have exactly 640 variables.
All inputs are finite; a program needn't handle non-finite values. Where the reference program divides by a largest or mean magnitude, that divisor is 1e-20 or more.
Results may differ from the reference program's by a relative error of at most 0.0038.
The reference program's roundings to bfloat16 on the way count: a program that leaves them out, or rounds other values in their place, can miss the bound.
Values may be sent and summed in bfloat16 or wider, within the bound.
No kernel may reach another device: no remote copies, remote signals or barrier semaphores. Data moves between devices by JAX's collectives and lax.ppermute only.
A program may use at most 64 MiB of HBM per device.

```python
import math
import jax
import jax.numpy as jnp
from jax import lax

CMAX = 512
ITERS = 5
LOW = 128
AVG = 320
NCG = 64
COMPS = 256
VG = 20480
V = 81920
ROWS = 1024


def group_sizes(key):
    base_key = jax.random.fold_in(key, 11)
    spread_key, shuffle_key, flip_key = jax.random.split(base_key, 3)
    group_total = COMPS // NCG
    pair_total = NCG // 2
    offsets = jax.random.randint(spread_key, (group_total, pair_total), 0, AVG - LOW + 1)
    offsets = offsets.at[:, 0].set(CMAX - AVG)
    shuffle_keys = jax.random.split(shuffle_key, group_total)
    offsets = jax.vmap(jax.random.permutation)(shuffle_keys, offsets)
    flips = jax.random.randint(flip_key, (group_total, pair_total), 0, 2) * 2 - 1
    signed = offsets * flips
    paired = jnp.stack([AVG + signed, AVG - signed], axis=2)
    return paired.reshape(group_total, NCG).astype(jnp.int32)


def draw_comp_sizes(key, part):
    return group_sizes(key).reshape(COMPS).astype(jnp.int32)


def draw_labels(key, part):
    group_total = COMPS // NCG
    sizes_table = group_sizes(key)
    ends = jnp.cumsum(sizes_table, axis=1)
    positions = jnp.arange(VG, dtype=jnp.int32)
    local_label = jnp.sum((positions[None, :, None] >= ends[:, None, :]).astype(jnp.int32), axis=2)
    shuffle_keys = jax.random.split(jax.random.fold_in(key, 13), group_total)
    shuffled = jax.vmap(jax.random.permutation)(shuffle_keys, local_label)
    group_offset = jnp.arange(group_total, dtype=jnp.int32)[:, None] * NCG
    return (shuffled + group_offset).reshape(V).astype(jnp.int32)


def draw_observed(key, part):
    base_key = jax.random.fold_in(key, 17)
    noise_key, column_key, row_key = jax.random.split(base_key, 3)
    column_trend = jnp.exp(math.log(3.0) * jnp.arange(V, dtype=jnp.float32) / V)
    row_trend = jnp.exp(math.log(3.0) * jnp.arange(ROWS, dtype=jnp.float32) / ROWS)
    noise = jnp.clip(jax.random.normal(noise_key, (ROWS, V), jnp.float32), -5.0, 5.0)
    column_rough = jnp.exp(jax.random.uniform(column_key, (V,), jnp.float32, 0.0, math.log(2.0)))
    row_rough = jnp.exp(jax.random.uniform(row_key, (ROWS,), jnp.float32, 0.0, math.log(2.0)))
    values = noise * (row_trend * row_rough)[:, None] * (column_trend * column_rough)[None, :]
    return values.astype(jnp.bfloat16)


def setup_inputs(seed: int = 0) -> dict:
    keys = jax.random.split(jax.random.key(seed), 4)
    observed = draw_observed(jax.random.fold_in(keys[3], 71), 0)
    labels = draw_labels(jax.random.fold_in(keys[3], 71), 0)
    comp_sizes = draw_comp_sizes(jax.random.fold_in(keys[3], 71), 0)
    return {"observed": observed, "labels": labels, "comp_sizes": comp_sizes}


shrink = 0.2
ridge = 0.5


def newton_inverse(matrix):
    identity = jnp.eye(matrix.shape[0], dtype=jnp.float32)
    row_bound = jnp.max(jnp.sum(jnp.abs(matrix), axis=1))
    current = identity / row_bound
    for sweep_index in range(ITERS):
        product = jnp.dot(matrix, current, precision=lax.Precision.HIGHEST)
        current = jnp.dot(current, 2.0 * identity - product, precision=lax.Precision.HIGHEST)
    return current


def reference(observed, labels, comp_sizes):
    row_count, var_count = observed.shape
    wide = observed.astype(jnp.float32)
    energy = jnp.sum(jnp.square(wide))
    average = energy / (row_count * var_count)

    def handle(result, component):
        columns = jnp.nonzero(labels == component, size=CMAX, fill_value=var_count)[0].astype(jnp.int32)
        live = (columns < var_count).astype(jnp.float32)
        safe = jnp.minimum(columns, var_count - 1).astype(jnp.int32)
        slot_block = jnp.take(wide, safe, axis=1) * live[None, :]
        covariance = jnp.dot(slot_block.T, slot_block, precision=lax.Precision.HIGHEST) / row_count
        target = jnp.trace(covariance) / comp_sizes[component].astype(jnp.float32)
        diag_lift = shrink * target + ridge * average
        matrix = (1.0 - shrink) * covariance + diag_lift * jnp.eye(CMAX, dtype=jnp.float32)
        inverse = newton_inverse(matrix).astype(jnp.bfloat16).astype(jnp.float32)
        mapped = jnp.dot(slot_block, inverse, precision=lax.Precision.HIGHEST)
        return result.at[:, columns].set(mapped, mode="drop"), None

    initial = jnp.zeros(observed.shape, jnp.float32)
    finished = lax.scan(handle, initial, jnp.arange(COMPS, dtype=jnp.int32))[0]
    return finished.astype(jnp.bfloat16)
```

```python
import functools

import jax
import jax.numpy as jnp
from jax import lax
from jax.experimental import pallas as pl
from jax.experimental.pallas import tpu as pltpu
from jax.sharding import Mesh
from jax.sharding import PartitionSpec as P

CMAX = 512
ITERS = 5
LO = 256
LANES = 128
SAMPLES = ("samples_0", "samples_1", "samples_2")
BF16 = jnp.bfloat16
F32 = jnp.float32

shrink = 0.2
ridge = 0.5


def iota(shape, axis):
    return lax.broadcasted_iota(jnp.int32, shape, axis)


def dot(a, b, contract=((1,), (0,))):
    return lax.dot_general(a, b, (contract, ((), ())), preferred_element_type=F32)


def halves(x):
    top = x.astype(BF16)
    return top, (x - top.astype(F32)).astype(BF16)


def partition_kernel(sizes_ref, labels_ref, x_ref, out_ref, rank_ref, lhs_ref, acc_ref, base_ref, energy_ref):
    rows, chunk = x_ref.shape
    comps = sizes_ref.shape[1]
    his = acc_ref.shape[0] // rows
    units = his * LO // (comps // 2) // LANES
    step = pl.program_id(0)

    @pl.when(step == 0)
    def _():
        slot = iota((comps, comps), 0)
        before = (iota((comps, comps), 1) == slot - 1) & (slot % 2 == 1)
        sizes = jnp.broadcast_to(sizes_ref[...], (comps, comps))
        lead = jnp.sum(jnp.where(before, sizes, 0).astype(F32), axis=1, keepdims=True)
        first = iota((comps, LO), 0) // 2 * (units * LANES)
        base_ref[...] = first.astype(F32) + jnp.broadcast_to(lead, (comps, LO))
        acc_ref[...] = jnp.zeros_like(acc_ref)
        energy_ref[...] = jnp.zeros_like(energy_ref)

    upper = jnp.where(iota((LO, LO), 0) < iota((LO, LO), 1), 1.0, 0.0).astype(BF16)
    base = base_ref[...]
    ranks = []
    for tile in range(chunk // LO):
        label = labels_ref[:, tile * LO : (tile + 1) * LO] % comps
        hot = jnp.where(iota((comps, LO), 0) == label, 1.0, 0.0)
        count = dot(hot.astype(BF16), upper)
        ranks.append(jnp.sum(hot * (base + count), axis=0, keepdims=True))
        base = base + (count[:, LO - 1 :] + hot[:, LO - 1 :])
    base_ref[...] = base
    rank = jnp.concatenate(ranks, axis=1).astype(jnp.int32)
    rank_ref[...] = rank
    hi = rank // LO
    lo = rank - hi * LO
    x = x_ref[...]
    wide = x.astype(F32)
    square = wide * wide
    energy_ref[...] += sum(
        square[r * 8 : (r + 1) * 8, c * LANES : (c + 1) * LANES]
        for r in range(rows // 8)
        for c in range(chunk // LANES)
    )
    hi_rows = jnp.broadcast_to(hi.astype(F32), (rows, chunk)).astype(BF16)
    for h in range(his):
        lhs_ref[h * rows : (h + 1) * rows, :] = jnp.where(
            hi_rows == jnp.asarray(h, BF16), x, jnp.zeros_like(x)
        )
    lo_hot = jnp.where(iota((LO, chunk), 0) == lo, 1.0, 0.0).astype(BF16)
    acc_ref[...] += dot(lhs_ref[...], lo_hot, ((1,), (1,)))

    @pl.when(step == pl.num_programs(0) - 1)
    def _():
        total = jnp.sum(jnp.sum(energy_ref[...], axis=0, keepdims=True), axis=1, keepdims=True)
        first = total.astype(BF16).astype(F32)
        second = (total - first).astype(BF16).astype(F32)
        third = total - first - second
        row = iota((8, LANES), 0)
        pieces = jnp.where(row == 0, first, jnp.where(row == 1, second, jnp.where(row == 2, third, 0.0)))
        pieces = pieces.astype(BF16)
        for slot in range(comps):
            pair, half = divmod(slot, 2)
            for u in range(units):
                h, side = divmod(pair * units + u, LO // LANES)
                start = h * rows + half * 8
                value = acc_ref[start : start + 8, side * LANES : (side + 1) * LANES]
                out_ref[slot, :, u * LANES : (u + 1) * LANES] = value.astype(BF16)
            out_ref[slot, :, units * LANES :] = pieces


def partition(sizes, labels, x, chunk=2048):
    rows, width = x.shape
    comps = sizes.shape[0]
    his = width // LO
    message = 2 * width // comps + LANES
    return pl.pallas_call(
        partition_kernel,
        grid=(width // chunk,),
        in_specs=[
            pl.BlockSpec((1, comps), lambda i: (0, 0)),
            pl.BlockSpec((1, chunk), lambda i: (0, i)),
            pl.BlockSpec((rows, chunk), lambda i: (0, i)),
        ],
        out_specs=[
            pl.BlockSpec((comps, rows // 2, message), lambda i: (0, 0, 0)),
            pl.BlockSpec((1, chunk), lambda i: (0, i)),
        ],
        out_shape=[
            jax.ShapeDtypeStruct((comps, rows // 2, message), BF16),
            jax.ShapeDtypeStruct((1, width), jnp.int32),
        ],
        scratch_shapes=[
            pltpu.VMEM((rows * his, chunk), BF16),
            pltpu.VMEM((rows * his, LO), F32),
            pltpu.VMEM((comps, LO), F32),
            pltpu.VMEM((8, LANES), F32),
        ],
        compiler_params=pltpu.CompilerParams(vmem_limit_bytes=48 << 20),
        name="partition",
    )(sizes.reshape(1, comps), labels.reshape(1, width), x)


def product(a, b):
    return dot(a[0], b[0]) + (dot(a[0], b[1]) + dot(a[1], b[0]))


def inverse_kernel(slot_ref, sizes_ref, energy_ref, own_ref, other_ref, out_ref, *, entries):
    rows = own_ref.shape[0]
    slot = slot_ref[0]
    half = slot % 2
    lead = sizes_ref[slot - half]
    bin_width = CMAX + LANES
    size = jnp.where(half == 0, lead, bin_width - lead)
    begin = jnp.where(half == 0, 0, lead - LANES)
    end = jnp.where(half == 0, lead, CMAX)
    place = iota((1, CMAX), 1)
    live = (place >= begin) & (place < end)
    frame = pl.ds(pl.multiple_of(half * LANES, LANES), CMAX)
    live_rows = jnp.broadcast_to(jnp.where(live, 1.0, 0.0), (rows, CMAX)).astype(BF16)
    own = own_ref[:, frame] * live_rows
    other = other_ref[:, frame] * live_rows
    gram = dot(own, own, ((0,), (0,))) + dot(other, other, ((0,), (0,)))
    covariance = gram * (1.0 / (2 * rows))
    diagonal = iota((CMAX, CMAX), 0) == iota((CMAX, CMAX), 1)

    def whole(value, reduce):
        return reduce(reduce(value, axis=0, keepdims=True), axis=1, keepdims=True)

    trace = whole(jnp.where(diagonal, covariance, 0.0), jnp.sum)
    average = jnp.max(energy_ref[...], axis=1, keepdims=True) * (1.0 / entries)
    lift = shrink * (trace / jnp.full((1, 1), size.astype(F32))) + ridge * average
    matrix = (1.0 - shrink) * covariance + jnp.where(diagonal, lift, 0.0)
    bound = whole(jnp.sum(jnp.abs(matrix), axis=0, keepdims=True), jnp.max)
    scale = 1.0 / bound
    error = jnp.where(diagonal, 1.0, 0.0) - matrix * scale
    total = jnp.where(diagonal, 1.0, 0.0) + error
    for _ in range(ITERS - 1):
        parts = halves(error)
        error = product(parts, parts)
        total = total + product(halves(total), halves(error))
    inverse = jnp.where(live, total * scale, 0.0)
    keep = jnp.broadcast_to(jnp.where(live, 1.0, 0.0), (8, CMAX))
    keep = jnp.sum(jnp.where(diagonal, keep[:1], 0.0), axis=1, keepdims=True)
    out_ref[...] = (inverse * keep).astype(BF16)


def component_inverse(slot, sizes, energy, own, other, entries):
    bin_width = CMAX + LANES
    rows = own.shape[0]
    vmem = pl.BlockSpec((rows, bin_width), lambda i: (0, 0))
    return pl.pallas_call(
        functools.partial(inverse_kernel, entries=entries),
        grid=(1,),
        in_specs=[
            pl.BlockSpec(memory_space=pltpu.SMEM),
            pl.BlockSpec(memory_space=pltpu.SMEM),
            pl.BlockSpec((1, LANES), lambda i: (0, 0)),
            vmem,
            vmem,
        ],
        out_specs=pl.BlockSpec((CMAX, CMAX), lambda i: (0, 0)),
        out_shape=jax.ShapeDtypeStruct((CMAX, CMAX), BF16),
        compiler_params=pltpu.CompilerParams(vmem_limit_bytes=48 << 20),
        name="component_inverse",
    )(slot, sizes, energy, own, other)


def whiten_kernel(slot_ref, rows_ref, own_ref, other_ref, out_ref):
    swap = slot_ref[0] % 2 == 1
    own = own_ref[...]
    other = other_ref[...]
    lead = jnp.where(swap, other, own)
    tail = jnp.where(swap, own, other)
    first = dot(rows_ref[:, :CMAX], lead)
    second = dot(rows_ref[:, LANES:], tail)
    out_ref[:, :LANES] = first[:, :LANES].astype(BF16)
    out_ref[:, LANES:CMAX] = (first[:, LANES:] + second[:, : CMAX - LANES]).astype(BF16)
    out_ref[:, CMAX:] = second[:, CMAX - LANES :].astype(BF16)


def whiten(slot, rows, own, other):
    bin_width = CMAX + LANES
    count = rows.shape[0]
    square = pl.BlockSpec((CMAX, CMAX), lambda i: (0, 0))
    return pl.pallas_call(
        whiten_kernel,
        grid=(1,),
        in_specs=[
            pl.BlockSpec(memory_space=pltpu.SMEM),
            pl.BlockSpec((count, bin_width), lambda i: (0, 0)),
            square,
            square,
        ],
        out_specs=pl.BlockSpec((count, bin_width), lambda i: (0, 0)),
        out_shape=jax.ShapeDtypeStruct((count, bin_width), BF16),
        compiler_params=pltpu.CompilerParams(vmem_limit_bytes=48 << 20),
        name="whiten",
    )(slot, rows, own, other)


def restore_kernel(rank_ref, bins_ref, out_ref, mat_ref):
    slots, half_rows, bin_width = bins_ref.shape
    rows, chunk = out_ref.shape
    units = bin_width // LANES
    his = mat_ref.shape[0] // rows

    @pl.when(pl.program_id(0) == 0)
    def _():
        for h in range(his):
            for side in range(LO // LANES):
                pair, u = divmod(h * (LO // LANES) + side, units)
                lanes = slice(u * LANES, (u + 1) * LANES)
                both = jnp.concatenate([bins_ref[2 * pair, :, lanes], bins_ref[2 * pair + 1, :, lanes]], axis=0)
                mat_ref[h * rows : (h + 1) * rows, side * LANES : (side + 1) * LANES] = both

    rank = rank_ref[...]
    hi = rank // LO
    lo = rank - hi * LO
    lo_hot = jnp.where(iota((LO, chunk), 0) == lo, 1.0, 0.0).astype(BF16)
    got = dot(mat_ref[...], lo_hot)
    hi_rows = jnp.broadcast_to(hi, (8, chunk))
    for s in range(0, rows, 8):
        value = got[s : s + 8]
        for h in range(1, his):
            value = jnp.where(hi_rows == h, got[h * rows + s : h * rows + s + 8], value)
        out_ref[s : s + 8, :] = value.astype(BF16)


def restore(rank, bins, chunk=1024):
    slots, half_rows, bin_width = bins.shape
    width = rank.shape[1]
    rows = 2 * half_rows
    return pl.pallas_call(
        restore_kernel,
        grid=(width // chunk,),
        in_specs=[
            pl.BlockSpec((1, chunk), lambda i: (0, i)),
            pl.BlockSpec(bins.shape, lambda i: (0, 0, 0)),
        ],
        out_specs=pl.BlockSpec((rows, chunk), lambda i: (0, i)),
        out_shape=jax.ShapeDtypeStruct((rows, width), BF16),
        scratch_shapes=[pltpu.VMEM((rows * (width // LO), LO), BF16)],
        compiler_params=pltpu.CompilerParams(vmem_limit_bytes=48 << 20),
        name="restore",
    )(rank, bins)


def partner(x):
    return lax.ppermute(x, "samples_2", [(0, 1), (1, 0)])


def body(observed, labels, comp_sizes):
    row_local, width_local = observed.shape
    slots = comp_sizes.shape[0]
    groups = lax.axis_size("groups")
    entries = row_local * lax.axis_size(SAMPLES) * width_local * groups
    slot = lax.axis_index(SAMPLES).astype(jnp.int32).reshape(1)
    message, rank = partition(comp_sizes, labels, observed)
    received = lax.all_to_all(message, SAMPLES, split_axis=0, concat_axis=0, tiled=True)
    energy = jnp.sum(received[:, :, CMAX + LANES :].astype(F32), axis=(0, 1)).reshape(1, LANES)
    shifted = [
        lax.ppermute(energy, "groups", [(i, (i + k) % groups) for i in range(groups)]) for k in range(1, groups)
    ]
    energy = sum(shifted, energy)
    rows = received.reshape(slots * (row_local // 2), -1)
    own = component_inverse(slot, comp_sizes, energy, rows, partner(rows), entries)
    mapped = whiten(slot, rows, own, partner(own))
    mapped = mapped.reshape(slots, row_local // 2, -1)
    returned = lax.all_to_all(mapped, SAMPLES, split_axis=0, concat_axis=0, tiled=True)
    return restore(rank, returned)


def solution(mesh):
    finer = Mesh(
        mesh.devices.reshape(8, 4, 2, mesh.shape["groups"]),
        ("samples_0", "samples_1", "samples_2", "groups"),
    )
    in_specs = (P(SAMPLES, "groups"), P("groups"), P("groups"))
    out_specs = P(SAMPLES, "groups")
    return jax.shard_map(body, mesh=finer, in_specs=in_specs, out_specs=out_specs, check_vma=False)
```

```python
import functools

import jax
import jax.numpy as jnp
from jax import lax
from jax.experimental import pallas as pl
from jax.experimental.pallas import tpu as pltpu
from jax.sharding import Mesh
from jax.sharding import PartitionSpec as P

CMAX = 512
ITERS = 5
LO = 256
LO_BITS = 8
PLACE_BITS = 10
LANES = 128
CHUNKS = 4
PIECE = 1024
SAMPLES = ("samples_0", "samples_1", "samples_2")
BF16 = jnp.bfloat16
F32 = jnp.float32

shrink = 0.2
ridge = 0.5


def iota(shape, axis):
    return lax.broadcasted_iota(jnp.int32, shape, axis)


def dot(a, b, contract=((1,), (0,))):
    return lax.dot_general(a, b, (contract, ((), ())), preferred_element_type=F32)


def halves(x):
    top = x.astype(BF16)
    return top, (x - top.astype(F32)).astype(BF16)


def one_hot_lo(place, ref):
    low = jnp.broadcast_to((place & (LO - 1)).astype(F32), (16, place.shape[1])).astype(BF16)
    level = iota((LO, LANES), 0).astype(F32).astype(BF16)
    for at in range(0, place.shape[1], LANES):
        lanes = slice(at, at + LANES)
        for r in range(0, LO, 16):
            same = level[r : r + 16] == low[:, lanes]
            ref[r : r + 16, lanes] = jnp.where(same, jnp.ones((16, LANES), BF16), jnp.zeros((16, LANES), BF16))


def window_of(begin):
    begin = jnp.concatenate([begin.astype(jnp.int32)] * (LO // LANES), axis=1)
    begin = jnp.broadcast_to(begin, (8, LO))
    return (begin >> LO_BITS) + jnp.where(iota((8, LO), 1) < (begin & (LO - 1)), 1, 0)


def bin_starts(start, bin_row):
    bins = start.shape[0]
    parts = []
    for at in range(0, bin_row.shape[1], LANES):
        same = iota((bins, LANES), 0) == bin_row[:, at : at + LANES]
        parts.append(jnp.sum(jnp.where(same, start, 0.0), axis=0, keepdims=True))
    return jnp.concatenate(parts, axis=1).astype(jnp.int32)


def partition_kernel(slot_ref, labels_ref, x_ref, out_ref, code_ref, start_ref, own_ref, lhs_ref, hot_ref, acc_ref):
    rows, width = x_ref.shape
    chunks, bins = start_ref.shape[0] - 1, start_ref.shape[1]
    chunk = width // chunks
    windows = acc_ref.shape[0]
    bin_width = own_ref.shape[1]
    units = bin_width // LANES
    pair = slot_ref[0] // 2

    label = labels_ref[...] & (2 * bins - 1)
    bin_row = label >> 1
    odd = label & 1
    upper = jnp.where(iota((LO, LO), 0) < iota((LO, LO), 1), 1.0, 0.0)
    counting = jnp.concatenate([upper, jnp.ones((LO, LANES), F32)], axis=1).astype(BF16)
    hots = [iota((bins, LO), 0) == bin_row[:, t : t + LO] for t in range(0, width, LO)]
    ones = jnp.concatenate([jnp.where(hot, 1.0, 0.0).astype(BF16) for hot in hots], axis=0)
    counts = dot(ones, counting)
    done = jnp.zeros((bins, LANES), F32)
    places = []
    most = jnp.zeros((bins, LANES), F32)
    for t, hot in enumerate(hots):
        if t * LO % chunk == 0:
            start_ref[t * LO // chunk] = done
        count = counts[t * bins : (t + 1) * bins]
        inside = jnp.concatenate([done] * (LO // LANES), axis=1) + count[:, :LO]
        places.append(jnp.sum(jnp.where(hot, inside, 0.0), axis=0, keepdims=True))
        done = done + count[:, LO:]
    start_ref[chunks] = done
    for c in range(chunks):
        most = jnp.maximum(most, start_ref[c + 1] - start_ref[c])
    longest = jnp.max(most)
    place = jnp.concatenate(places, axis=1).astype(jnp.int32)
    code_ref[...] = (bin_row << PLACE_BITS) + place

    def masked(c, bin_now, ref):
        columns = slice(c * chunk, (c + 1) * chunk)
        x = x_ref[:, columns]
        bin_rows = jnp.broadcast_to(bin_now.astype(F32), (rows, chunk)).astype(BF16)
        for p in range(bins):
            ref[p * rows : (p + 1) * rows, :] = jnp.where(
                bin_rows == jnp.asarray(p, BF16), x, jnp.zeros_like(x)
            )
        mine = jnp.where(bin_now == pair, odd[:, columns], 0).astype(F32)
        ref[bins * rows :, :] = jnp.broadcast_to(mine, (rows, chunk)).astype(BF16)

    def first_places(c, p):
        if p < bins:
            return start_ref[c, p : p + 1, :]
        return start_ref[c, pl.ds(pair, 1), :]

    runs = []
    for c in range(chunks):
        columns = slice(c * chunk, (c + 1) * chunk)
        one_hot_lo(place[:, columns], hot_ref.at[c])
        masked(c, bin_row[:, columns], lhs_ref.at[c])
        runs.append(dot(lhs_ref[c], hot_ref[c], ((1,), (1,))))

    total = jnp.zeros((8, LANES), F32)
    for at in range(0, width, LANES):
        wide = x_ref[:, at : at + LANES].astype(F32)
        square = wide * wide
        for r in range(0, rows, 8):
            total = total + square[r : r + 8]
    total = whole(total, jnp.sum)
    first = total.astype(BF16).astype(F32)
    second = (total - first).astype(BF16).astype(F32)
    third = total - first - second
    row = iota((8, LANES), 0)
    pieces = jnp.where(row == 0, first, jnp.where(row == 1, second, jnp.where(row == 2, third, 0.0)))
    pieces = pieces.astype(BF16)

    for p in range(bins + 1):
        reached = [window_of(first_places(c, p)) for c in range(chunks)]
        for w in range(windows):
            hits = [window == w for window in reached]
            for half in range(2 if p < bins else 1):
                r = p * rows + half * 8
                value = jnp.where(hits[0], runs[0][r : r + 8], 0.0)
                for hit, run in zip(hits[1:], runs[1:]):
                    value = jnp.where(hit, run[r : r + 8], value)
                for side in range(LO // LANES):
                    u = w * (LO // LANES) + side
                    if u >= units:
                        continue
                    piece = value[:, side * LANES : (side + 1) * LANES]
                    if p < bins:
                        out_ref[2 * p + half, :, u * LANES : (u + 1) * LANES] = piece.astype(BF16)
                    else:
                        own_ref[:, u * LANES : (u + 1) * LANES] = piece
    for s in range(2 * bins):
        out_ref[s, :, bin_width:] = pieces

    @pl.when(longest > LO)
    def _():
        acc_ref[...] = jnp.zeros_like(acc_ref)
        passes = longest.astype(jnp.int32) // LO + 1
        for c in range(chunks):
            columns = slice(c * chunk, (c + 1) * chunk)
            now = (code_ref[:, columns] >> PLACE_BITS)
            turn = ((code_ref[:, columns] & (2**PLACE_BITS - 1)) - bin_starts(start_ref[c], now)) >> LO_BITS

            def one_pass(k, carry, c=c, now=now, turn=turn):
                masked(c, jnp.where(turn == k, now, -1), lhs_ref.at[c])
                got = dot(lhs_ref[c], hot_ref[c], ((1,), (1,)))
                for p in range(bins + 1):
                    window = window_of(first_places(c, p) + (k * LO).astype(F32))
                    for w in range(windows):
                        for r in range(p * rows, (p + 1) * rows, 8):
                            acc_ref[w, r : r + 8] += jnp.where(window == w, got[r : r + 8], 0.0)
                return carry

            lax.fori_loop(0, passes, one_pass, 0)
        for u in range(units):
            w, side = divmod(u, LO // LANES)
            lanes = slice(side * LANES, (side + 1) * LANES)
            own_ref[:, u * LANES : (u + 1) * LANES] = acc_ref[w, bins * rows : bins * rows + 8, lanes]
            for s in range(2 * bins):
                out_ref[s, :, u * LANES : (u + 1) * LANES] = acc_ref[w, s * 8 : s * 8 + 8, lanes].astype(BF16)


def partition(slot, comps, labels, x, chunks=CHUNKS):
    rows, width = x.shape
    bins = comps // 2
    bin_width = width // bins
    windows = -(-bin_width // LO)
    chunk = width // chunks
    outs = [
        jax.ShapeDtypeStruct((comps, rows // 2, bin_width + LANES), BF16),
        jax.ShapeDtypeStruct((1, width), jnp.int32),
        jax.ShapeDtypeStruct((chunks + 1, bins, LANES), F32),
        jax.ShapeDtypeStruct((8, bin_width), F32),
    ]
    scratch = [
        pltpu.VMEM((chunks, (bins + 1) * rows, chunk), BF16),
        pltpu.VMEM((chunks, LO, chunk), BF16),
        pltpu.VMEM((windows, (bins + 1) * rows, LO), F32),
    ]
    return on_core(partition_kernel, "partition", outs, [slot], [labels.reshape(1, width), x], scratch=scratch)


def product(a, b):
    return dot(a[0], b[0]) + (dot(a[0], b[1]) + dot(a[1], b[0]))


def whole(value, reduce):
    return reduce(reduce(value, axis=0, keepdims=True), axis=1, keepdims=True)


def compaction(odd_ref, parity):
    bin_width = odd_ref.shape[1]
    mine = odd_ref[...] == parity.astype(F32)
    before = jnp.where(iota((bin_width, bin_width), 0) < iota((bin_width, bin_width), 1), 1.0, 0.0)
    place = dot(jnp.where(mine, 1.0, 0.0).astype(BF16), before.astype(BF16))
    place = jnp.where(mine, place, -1.0)[:1].astype(jnp.int32)
    return jnp.where(iota((CMAX, bin_width), 0) == place, 1.0, 0.0).astype(BF16)


def gram_kernel(slot_ref, odd_ref, own_ref, other_ref, out_ref):
    pick = compaction(odd_ref, slot_ref[0] % 2)
    total = None
    for ref in (own_ref, other_ref):
        x = dot(ref[...], pick, ((1,), (1,))).astype(BF16)
        part = dot(x, x, ((0,), (0,)))
        total = part if total is None else total + part
    out_ref[...] = total


def inverse_kernel(slot_ref, sizes_ref, energy_ref, gram_ref, out_ref, *, row_count, entries):
    size = sizes_ref[slot_ref[0]]
    covariance = gram_ref[...] * (1.0 / row_count)
    diagonal = iota((CMAX, CMAX), 0) == iota((CMAX, CMAX), 1)
    trace = whole(jnp.where(diagonal, covariance, 0.0), jnp.sum)
    average = jnp.max(energy_ref[...], axis=1, keepdims=True) * (1.0 / entries)
    lift = shrink * (trace / jnp.full((1, 1), size.astype(F32))) + ridge * average
    matrix = (1.0 - shrink) * covariance + jnp.where(diagonal, lift, 0.0)
    bound = whole(jnp.sum(jnp.abs(matrix), axis=0, keepdims=True), jnp.max)
    scale = 1.0 / bound
    error = jnp.where(diagonal, 1.0, 0.0) - matrix * scale
    total = jnp.where(diagonal, 1.0, 0.0) + error
    for _ in range(ITERS - 1):
        parts = halves(error)
        error = product(parts, parts)
        total = total + product(halves(total), halves(error))
    out_ref[...] = (total * scale).astype(BF16)


def whiten_own_kernel(slot_ref, odd_ref, rows_ref, inverse_ref, done_ref, next_ref):
    parity = slot_ref[0] % 2
    pick = compaction(odd_ref, parity)
    rows = rows_ref[...]
    x = dot(rows, pick, ((1,), (1,))).astype(BF16)
    mapped = dot(x, inverse_ref[...]).astype(BF16)
    done_ref[...] = dot(mapped, pick).astype(BF16)
    next_ref[...] = dot(rows, compaction(odd_ref, 1 - parity), ((1,), (1,))).astype(BF16)


def whiten_other_kernel(slot_ref, odd_ref, done_ref, x_ref, inverse_ref, out_ref):
    pick = compaction(odd_ref, 1 - slot_ref[0] % 2)
    mapped = dot(x_ref[...], inverse_ref[...]).astype(BF16)
    out_ref[...] = (done_ref[...].astype(F32) + dot(mapped, pick)).astype(BF16)


def on_core(kernel, name, outs, scalars, arrays, blocks=None, scratch=()):
    blocks = blocks or {}

    def spec(shape):
        return pl.BlockSpec(shape, lambda i: (0,) * len(shape))

    specs = [pl.BlockSpec(memory_space=pltpu.SMEM) for _ in scalars]
    specs += [spec(blocks.get(place, array.shape)) for place, array in enumerate(arrays)]
    return pl.pallas_call(
        kernel,
        grid=(1,),
        in_specs=specs,
        out_specs=[spec(out.shape) for out in outs],
        out_shape=outs,
        scratch_shapes=list(scratch),
        compiler_params=pltpu.CompilerParams(vmem_limit_bytes=56 << 20),
        name=name,
    )(*scalars, *arrays)


def restore_kernel(code_ref, start_ref, bins_ref, out_ref, mat_ref, lhs_ref, hot_ref):
    slots, half_rows, bin_width = bins_ref.shape
    rows, width = out_ref.shape
    bins = slots // 2
    chunks = start_ref.shape[0] - 1
    chunk = width // chunks
    units = bin_width // LANES
    windows = mat_ref.shape[0]

    for w in range(windows):
        for side in range(LO // LANES):
            u = w * (LO // LANES) + side
            lanes = slice(side * LANES, (side + 1) * LANES)
            for s in range(slots):
                if u < units:
                    piece = bins_ref[s, :, u * LANES : (u + 1) * LANES].astype(F32)
                else:
                    piece = jnp.zeros((half_rows, LANES), F32)
                mat_ref[w, s * half_rows : (s + 1) * half_rows, lanes] = piece
    code = code_ref[...]
    bin_row = code >> PLACE_BITS
    most = start_ref[1] - start_ref[0]
    for c in range(1, chunks):
        most = jnp.maximum(most, start_ref[c + 1] - start_ref[c])
    longest = jnp.max(most)

    def runs(c, shift, ref):
        for p in range(bins):
            window = window_of(start_ref[c, p : p + 1, :] + shift)
            pieces = []
            for r in range(p * rows, (p + 1) * rows, 8):
                value = mat_ref[0, r : r + 8]
                for w in range(1, windows):
                    value = jnp.where(window == w, mat_ref[w, r : r + 8], value)
                pieces.append(value)
            ref[p * rows : (p + 1) * rows] = jnp.concatenate(pieces, axis=0).astype(BF16)

    def choose(lhs, at, bin_now, old):
        lanes = slice(at, at + PIECE)
        got = dot(lhs, hot_ref[:, lanes])
        bin_rows = jnp.broadcast_to(bin_now, (8, PIECE))
        for s in range(0, rows, 8):
            value = got[s : s + 8] if old is None else old[s : s + 8]
            for p in range(1 if old is None else 0, bins):
                value = jnp.where(bin_rows == p, got[p * rows + s : p * rows + s + 8], value)
            out_ref[s : s + 8, lanes] = value.astype(BF16)

    for c in range(chunks):
        columns = slice(c * chunk, (c + 1) * chunk)
        one_hot_lo(code[:, columns], hot_ref.at[:, columns])
        runs(c, 0.0, lhs_ref.at[c])
        lhs = lhs_ref[c]
        for at in range(c * chunk, (c + 1) * chunk, PIECE):
            choose(lhs, at, bin_row[:, at : at + PIECE], None)

    @pl.when(longest > LO)
    def _():
        passes = longest.astype(jnp.int32) // LO + 1
        for c in range(chunks):

            def one_pass(k, carry, c=c):
                runs(c, (k * LO).astype(F32), lhs_ref.at[c])
                lhs = lhs_ref[c]
                for at in range(c * chunk, (c + 1) * chunk, PIECE):
                    lanes = slice(at, at + PIECE)
                    part = code_ref[:, lanes]
                    now = part >> PLACE_BITS
                    turn = ((part & (2**PLACE_BITS - 1)) - bin_starts(start_ref[c], now)) >> LO_BITS
                    choose(lhs, at, jnp.where(turn == k, now, -1), out_ref[:, lanes].astype(F32))
                return carry

            lax.fori_loop(0, passes, one_pass, 0)


def restore(code, start, bins):
    slots, half_rows, bin_width = bins.shape
    width = code.shape[1]
    chunks = start.shape[0] - 1
    windows = -(-bin_width // LO)
    scratch = [
        pltpu.VMEM((windows, slots * half_rows, LO), F32),
        pltpu.VMEM((chunks, slots * half_rows, LO), BF16),
        pltpu.VMEM((LO, width), BF16),
    ]
    outs = [jax.ShapeDtypeStruct((2 * half_rows, width), BF16)]
    return on_core(restore_kernel, "restore", outs, [], [code, start, bins], scratch=scratch)[0]


def partner(x):
    return lax.ppermute(x, "samples_2", [(0, 1), (1, 0)])


def body(observed, labels, comp_sizes):
    row_local, width_local = observed.shape
    slots = comp_sizes.shape[0]
    groups = lax.axis_size("groups")
    row_count = row_local * lax.axis_size(SAMPLES)
    slot = lax.axis_index(SAMPLES).astype(jnp.int32).reshape(1)
    message, code, start, odd = partition(slot, slots, labels, observed)
    received = lax.all_to_all(message, SAMPLES, split_axis=0, concat_axis=0, tiled=True)
    bin_width = odd.shape[1]
    energy = jnp.sum(received[:, :, bin_width:].astype(F32), axis=(0, 1)).reshape(1, LANES)
    shifted = [
        lax.ppermute(energy, "groups", [(i, (i + k) % groups) for i in range(groups)]) for k in range(1, groups)
    ]
    energy = sum(shifted, energy)
    rows = received.reshape(row_count // 2, -1)
    use = (row_count // 2, bin_width)
    square = jax.ShapeDtypeStruct((CMAX, CMAX), F32)
    narrow = jax.ShapeDtypeStruct((CMAX, CMAX), BF16)
    tall = jax.ShapeDtypeStruct((row_count // 2, CMAX), BF16)
    flat = jax.ShapeDtypeStruct(use, BF16)
    (gram,) = on_core(gram_kernel, "gram", [square], [slot], [odd, rows, partner(rows)], {1: use, 2: use})
    newton = functools.partial(
        inverse_kernel, row_count=row_count, entries=row_count * width_local * groups
    )
    (own,) = on_core(newton, "inverse", [narrow], [slot, comp_sizes], [energy, gram])
    other = partner(own)
    done, waiting = on_core(whiten_own_kernel, "whiten_own", [flat, tall], [slot], [odd, rows, own], {1: use})
    (mapped,) = on_core(whiten_other_kernel, "whiten_other", [flat], [slot], [odd, done, waiting, other])
    mapped = mapped.reshape(slots, row_local // 2, -1)
    returned = lax.all_to_all(mapped, SAMPLES, split_axis=0, concat_axis=0, tiled=True)
    return restore(code, start, returned)


def solution(mesh):
    finer = Mesh(
        mesh.devices.reshape(8, 4, 2, mesh.shape["groups"]),
        ("samples_0", "samples_1", "samples_2", "groups"),
    )
    in_specs = (P(SAMPLES, "groups"), P("groups"), P("groups"))
    out_specs = P(SAMPLES, "groups")
    return jax.shard_map(body, mesh=finer, in_specs=in_specs, out_specs=out_specs, check_vma=False)
```

```python
import functools

import jax
import jax.numpy as jnp
from jax import lax
from jax.experimental import pallas as pl
from jax.experimental.pallas import tpu as pltpu
from jax.sharding import Mesh
from jax.sharding import PartitionSpec as P

CMAX = 512
ITERS = 5
LO = 256
LO_BITS = 8
PLACE_BITS = 10
LANES = 128
CHUNKS = 4
PIECE = 1024
CHIPS = ("samples_0", "samples_1")
SAMPLES = ("samples_0", "samples_1", "samples_2")
BF16 = jnp.bfloat16
F32 = jnp.float32

shrink = 0.2
ridge = 0.5


def iota(shape, axis):
    return lax.broadcasted_iota(jnp.int32, shape, axis)


def dot(a, b, contract=((1,), (0,))):
    return lax.dot_general(a, b, (contract, ((), ())), preferred_element_type=F32)


def halves(x):
    top = x.astype(BF16)
    return top, (x - top.astype(F32)).astype(BF16)


def one_hot_lo(place, ref):
    low = jnp.broadcast_to((place & (LO - 1)).astype(F32), (16, place.shape[1])).astype(BF16)
    level = iota((LO, LANES), 0).astype(F32).astype(BF16)
    for at in range(0, place.shape[1], LANES):
        lanes = slice(at, at + LANES)
        for r in range(0, LO, 16):
            same = level[r : r + 16] == low[:, lanes]
            ref[r : r + 16, lanes] = jnp.where(same, jnp.ones((16, LANES), BF16), jnp.zeros((16, LANES), BF16))


def window_of(begin):
    begin = jnp.concatenate([begin.astype(jnp.int32)] * (LO // LANES), axis=1)
    begin = jnp.broadcast_to(begin, (8, LO))
    return (begin >> LO_BITS) + jnp.where(iota((8, LO), 1) < (begin & (LO - 1)), 1, 0)


def bin_starts(start, bin_row):
    bins = start.shape[0]
    parts = []
    for at in range(0, bin_row.shape[1], LANES):
        same = iota((bins, LANES), 0) == bin_row[:, at : at + LANES]
        parts.append(jnp.sum(jnp.where(same, start, 0.0), axis=0, keepdims=True))
    return jnp.concatenate(parts, axis=1).astype(jnp.int32)


def partition_kernel(slot_ref, labels_ref, x_ref, out_ref, code_ref, start_ref, own_ref, lhs_ref, hot_ref, acc_ref):
    rows, width = x_ref.shape
    chunks, bins = start_ref.shape[0] - 1, start_ref.shape[1]
    chunk = width // chunks
    windows = acc_ref.shape[0]
    bin_width = own_ref.shape[1]
    units = bin_width // LANES
    pair = slot_ref[0] // 2

    label = labels_ref[...] & (2 * bins - 1)
    bin_row = label >> 1
    upper = jnp.where(iota((LO, LO), 0) < iota((LO, LO), 1), 1.0, 0.0)
    counting = jnp.concatenate([upper, jnp.ones((LO, LANES), F32)], axis=1).astype(BF16)
    hots = [iota((bins, LO), 0) == bin_row[:, t : t + LO] for t in range(0, width, LO)]
    ones = jnp.concatenate([jnp.where(hot, 1.0, 0.0).astype(BF16) for hot in hots], axis=0)
    counts = dot(ones, counting)
    done = jnp.zeros((bins, LANES), F32)
    places = []
    most = jnp.zeros((bins, LANES), F32)
    for t, hot in enumerate(hots):
        if t * LO % chunk == 0:
            start_ref[t * LO // chunk] = done
        count = counts[t * bins : (t + 1) * bins]
        inside = jnp.concatenate([done] * (LO // LANES), axis=1) + count[:, :LO]
        places.append(jnp.sum(jnp.where(hot, inside, 0.0), axis=0, keepdims=True))
        done = done + count[:, LO:]
    start_ref[chunks] = done
    for c in range(chunks):
        most = jnp.maximum(most, start_ref[c + 1] - start_ref[c])
    longest = jnp.max(most)
    place = jnp.concatenate(places, axis=1).astype(jnp.int32)
    code_ref[...] = (bin_row << PLACE_BITS) + place

    def masked(c, bin_now, ref):
        columns = slice(c * chunk, (c + 1) * chunk)
        if not isinstance(c, int):
            columns = pl.ds(pl.multiple_of(c * chunk, chunk), chunk)
        x = x_ref[:, columns]
        bin_rows = jnp.broadcast_to(bin_now.astype(F32), (rows, chunk)).astype(BF16)
        for p in range(bins):
            ref[p * rows : (p + 1) * rows, :] = jnp.where(
                bin_rows == jnp.asarray(p, BF16), x, jnp.zeros_like(x)
            )
        mine = jnp.where(bin_now == pair, labels_ref[:, columns] & 1, 0).astype(F32)
        ref[bins * rows :, :] = jnp.broadcast_to(mine, (rows, chunk)).astype(BF16)

    def first_places(c, p):
        if p < bins:
            return start_ref[c, p : p + 1, :]
        return start_ref[c, pl.ds(pair, 1), :]

    runs = []
    for c in range(chunks):
        columns = slice(c * chunk, (c + 1) * chunk)
        one_hot_lo(place[:, columns], hot_ref.at[c])
        masked(c, bin_row[:, columns], lhs_ref.at[c])
        runs.append(dot(lhs_ref[c], hot_ref[c], ((1,), (1,))))

    total = jnp.zeros((8, LANES), F32)
    for at in range(0, width, LANES):
        wide = x_ref[:, at : at + LANES].astype(F32)
        square = wide * wide
        for r in range(0, rows, 8):
            total = total + square[r : r + 8]
    total = whole(total, jnp.sum)
    first = total.astype(BF16).astype(F32)
    second = (total - first).astype(BF16).astype(F32)
    third = total - first - second
    row = iota((8, LANES), 0)
    pieces = jnp.where(row == 0, first, jnp.where(row == 1, second, jnp.where(row == 2, third, 0.0)))
    pieces = pieces.astype(BF16)

    for p in range(bins + 1):
        reached = [window_of(first_places(c, p)) for c in range(chunks)]
        for w in range(windows):
            hits = [window == w for window in reached]
            for half in range(2 if p < bins else 1):
                r = p * rows + half * 8
                value = jnp.where(hits[0], runs[0][r : r + 8], 0.0)
                for hit, run in zip(hits[1:], runs[1:]):
                    value = jnp.where(hit, run[r : r + 8], value)
                for side in range(LO // LANES):
                    u = w * (LO // LANES) + side
                    if u >= units:
                        continue
                    piece = value[:, side * LANES : (side + 1) * LANES]
                    if p < bins:
                        at = half * bin_width + u * LANES
                        out_ref[p, :, at : at + LANES] = piece.astype(BF16)
                    else:
                        own_ref[:, u * LANES : (u + 1) * LANES] = piece
    for p in range(bins):
        out_ref[p, :, 2 * bin_width :] = pieces

    @pl.when(longest > LO)
    def _():
        acc_ref[...] = jnp.zeros_like(acc_ref)
        passes = longest.astype(jnp.int32) // LO + 1

        def one_chunk(c, carry):
            code = code_ref[:, pl.ds(pl.multiple_of(c * chunk, chunk), chunk)]
            now = code >> PLACE_BITS
            code = code & (2**PLACE_BITS - 1)
            turn = (code - bin_starts(start_ref[c], now)) >> LO_BITS

            def one_pass(k, carry):
                masked(c, jnp.where(turn == k, now, -1), lhs_ref.at[0])
                got = dot(lhs_ref[0], hot_ref[c], ((1,), (1,)))
                for p in range(bins + 1):
                    window = window_of(first_places(c, p) + (k * LO).astype(F32))
                    for w in range(windows):
                        for r in range(p * rows, (p + 1) * rows, 8):
                            acc_ref[w, r : r + 8] += jnp.where(window == w, got[r : r + 8], 0.0)
                return carry

            return lax.fori_loop(0, passes, one_pass, carry)

        lax.fori_loop(0, chunks, one_chunk, 0)
        for u in range(units):
            w, side = divmod(u, LO // LANES)
            lanes = slice(side * LANES, (side + 1) * LANES)
            own_ref[:, u * LANES : (u + 1) * LANES] = acc_ref[w, bins * rows : bins * rows + 8, lanes]
            for s in range(2 * bins):
                at = s % 2 * bin_width + u * LANES
                out_ref[s // 2, :, at : at + LANES] = acc_ref[w, s * 8 : s * 8 + 8, lanes].astype(BF16)

    below = jnp.where(iota((LANES, LANES), 0) < iota((LANES, LANES), 1), 1.0, 0.0)
    below = jnp.concatenate([below, jnp.ones((LANES, LANES), F32)], axis=1).astype(BF16)
    so_far = jnp.zeros((8, LANES), F32)
    row = iota((8, LANES), 0)
    for u in range(units):
        lanes = slice(u * LANES, (u + 1) * LANES)
        odds = own_ref[:, lanes]
        count = dot(odds.astype(BF16), below)
        place_odd = so_far + count[:, :LANES]
        place_even = (iota((8, LANES), 1) + u * LANES).astype(F32) - place_odd
        so_far = so_far + count[:, LANES:]
        own_ref[:, lanes] = jnp.where(
            row == 0, jnp.where(odds == 0.0, place_even, -1.0), jnp.where(odds == 1.0, place_odd, -1.0)
        )


def partition(slot, comps, labels, x, chunks=CHUNKS):
    rows, width = x.shape
    bins = comps // 2
    bin_width = width // bins
    windows = -(-bin_width // LO)
    chunk = width // chunks
    outs = [
        jax.ShapeDtypeStruct((bins, rows // 2, 2 * bin_width + LANES), BF16),
        jax.ShapeDtypeStruct((1, width), jnp.int32),
        jax.ShapeDtypeStruct((chunks + 1, bins, LANES), F32),
        jax.ShapeDtypeStruct((8, bin_width), F32),
    ]
    scratch = [
        pltpu.VMEM((chunks, (bins + 1) * rows, chunk), BF16),
        pltpu.VMEM((chunks, LO, chunk), BF16),
        pltpu.VMEM((windows, (bins + 1) * rows, LO), F32),
    ]
    return on_core(partition_kernel, "partition", outs, [slot], [labels.reshape(1, width), x], 48, scratch)


def product(a, b):
    return dot(a[0], b[0]) + (dot(a[0], b[1]) + dot(a[1], b[0]))


def whole(value, reduce):
    return reduce(reduce(value, axis=0, keepdims=True), axis=1, keepdims=True)


def compaction(places_ref, parity):
    place = places_ref[pl.ds(parity, 1), :].astype(jnp.int32)
    return jnp.where(iota((CMAX, places_ref.shape[1]), 0) == place, 1.0, 0.0).astype(BF16)


def groups_of_rows(ref, bin_width):
    for at in (0, bin_width):
        block = ref[:, :, at : at + bin_width]
        yield block.reshape(block.shape[0] * block.shape[1], bin_width)


def gram_kernel(slot_ref, places_ref, own_ref, other_ref, gram_ref, x_ref, energy_ref):
    bin_width = places_ref.shape[1]
    pick = compaction(places_ref, slot_ref[0] % 2)
    total = None
    at = 0
    for ref in (own_ref, other_ref):
        for block in groups_of_rows(ref, bin_width):
            x = dot(block, pick, ((1,), (1,))).astype(BF16)
            if at < x_ref.shape[0]:
                x_ref[at : at + x.shape[0], :] = x
                at += x.shape[0]
            part = dot(x, x, ((0,), (0,)))
            total = part if total is None else total + part
    gram_ref[...] = total
    energy_ref[...] = sum(jnp.sum(ref[:, :, 2 * bin_width :].astype(F32), axis=0) for ref in (own_ref, other_ref))


def powers_kernel(gram_ref, low_ref, high_ref, last_ref, sums_ref, *, row_count):
    covariance = gram_ref[...] * (1.0 / row_count)
    diagonal = iota((CMAX, CMAX), 0) == iota((CMAX, CMAX), 1)
    trace = whole(jnp.where(diagonal, covariance, 0.0), jnp.sum)
    shrunk = (1.0 - shrink) * covariance
    bound = whole(jnp.sum(jnp.abs(shrunk), axis=0, keepdims=True), jnp.max)
    base = jnp.where(diagonal, 1.0, 0.0) - shrunk * (1.0 / jnp.maximum(bound, 1e-30))
    row = iota((8, LANES), 0)
    sums_ref[...] = jnp.where(row == 0, trace, bound)
    for ref in (low_ref, high_ref):
        parts = halves(base)
        square = product(parts, parts)
        squares = halves(square)
        ref[0] = base
        ref[1] = square
        ref[2] = product(squares, parts)
        base = product(squares, squares)
    top, rest = halves(base)
    last_ref[0] = top
    last_ref[1] = rest


def inverse_kernel(slot_ref, sizes_ref, e0_ref, e1_ref, e2_ref, e3_ref, sums_ref, low_ref, high_ref, last_ref, out_ref, *, entries):
    size = sizes_ref[slot_ref[0]]
    energy = e0_ref[...] + e1_ref[...] + e2_ref[...] + e3_ref[...]
    average = (energy[0:1, :1] + energy[1:2, :1] + energy[2:3, :1]) * (1.0 / entries)
    trace, bound = sums_ref[0:1, :1], sums_ref[1:2, :1]
    lift = shrink * (trace / jnp.full((1, 1), size.astype(F32))) + ridge * average
    scale = 1.0 / (bound + lift)
    theta = bound * scale
    diagonal = jnp.where(iota((CMAX, CMAX), 0) == iota((CMAX, CMAX), 1), 1.0, 0.0)
    t2 = theta * theta
    t4 = t2 * t2
    t8 = t4 * t4
    low = diagonal + theta * low_ref[0] + t2 * low_ref[1] + (theta * t2) * low_ref[2]
    high = diagonal + t4 * high_ref[0] + t8 * high_ref[1] + (t4 * t8) * high_ref[2]
    total = product(halves(low), halves(high))
    total = total + (t8 * t8) * product(halves(total), (last_ref[0], last_ref[1]))
    out_ref[...] = (total * scale).astype(BF16)


def whiten_own_kernel(slot_ref, places_ref, rows_ref, x_ref, inverse_ref, done_ref, next_ref):
    parity = slot_ref[0] % 2
    bin_width = places_ref.shape[1]
    mapped = dot(x_ref[...], inverse_ref[...]).astype(BF16)
    done_ref[...] = dot(mapped, compaction(places_ref, parity)).astype(BF16)
    pick = compaction(places_ref, 1 - parity)
    at = 0
    for block in groups_of_rows(rows_ref, bin_width):
        next_ref[at : at + block.shape[0], :] = dot(block, pick, ((1,), (1,))).astype(BF16)
        at += block.shape[0]


def whiten_other_kernel(slot_ref, places_ref, done_ref, x_ref, inverse_ref, out_ref):
    pick = compaction(places_ref, 1 - slot_ref[0] % 2)
    mapped = dot(x_ref[...], inverse_ref[...]).astype(BF16)
    value = (done_ref[...].astype(F32) + dot(mapped, pick)).astype(BF16)
    count, bin_width = value.shape[0] // 2, value.shape[1]
    for half in range(2):
        block = value[half * count : (half + 1) * count].reshape(out_ref.shape[0], out_ref.shape[1], bin_width)
        out_ref[:, :, half * bin_width : (half + 1) * bin_width] = block


def on_core(kernel, name, outs, scalars, arrays, mebibytes, scratch=()):
    def spec(shape):
        return pl.BlockSpec(shape, lambda i: (0,) * len(shape))

    return pl.pallas_call(
        kernel,
        grid=(1,),
        in_specs=[pl.BlockSpec(memory_space=pltpu.SMEM) for _ in scalars] + [spec(a.shape) for a in arrays],
        out_specs=[spec(out.shape) for out in outs],
        out_shape=outs,
        scratch_shapes=list(scratch),
        compiler_params=pltpu.CompilerParams(vmem_limit_bytes=mebibytes << 20),
        name=name,
    )(*scalars, *arrays)


def restore_kernel(code_ref, start_ref, bins_ref, out_ref, mat_ref, lhs_ref, hot_ref):
    bins, half_rows, bin_width = bins_ref.shape
    bin_width = bin_width // 2
    rows, width = out_ref.shape
    slots = 2 * bins
    chunks = start_ref.shape[0] - 1
    chunk = width // chunks
    units = bin_width // LANES
    windows = mat_ref.shape[0]

    for w in range(windows):
        for side in range(LO // LANES):
            u = w * (LO // LANES) + side
            lanes = slice(side * LANES, (side + 1) * LANES)
            for s in range(slots):
                if u < units:
                    at = s % 2 * bin_width + u * LANES
                    piece = bins_ref[s // 2, :, at : at + LANES].astype(F32)
                else:
                    piece = jnp.zeros((half_rows, LANES), F32)
                mat_ref[w, s * half_rows : (s + 1) * half_rows, lanes] = piece
    code = code_ref[...]
    bin_row = code >> PLACE_BITS
    most = start_ref[1] - start_ref[0]
    for c in range(1, chunks):
        most = jnp.maximum(most, start_ref[c + 1] - start_ref[c])
    longest = jnp.max(most)

    def runs(c, shift, ref):
        for p in range(bins):
            window = window_of(start_ref[c, p : p + 1, :] + shift)
            pieces = []
            for r in range(p * rows, (p + 1) * rows, 8):
                value = mat_ref[0, r : r + 8]
                for w in range(1, windows):
                    value = jnp.where(window == w, mat_ref[w, r : r + 8], value)
                pieces.append(value)
            ref[p * rows : (p + 1) * rows] = jnp.concatenate(pieces, axis=0).astype(BF16)

    def choose(lhs, lanes, bin_now, old):
        got = dot(lhs, hot_ref[:, lanes])
        bin_rows = jnp.broadcast_to(bin_now, (8, PIECE))
        for s in range(0, rows, 8):
            value = got[s : s + 8] if old is None else old[s : s + 8]
            for p in range(1 if old is None else 0, bins):
                value = jnp.where(bin_rows == p, got[p * rows + s : p * rows + s + 8], value)
            out_ref[s : s + 8, lanes] = value.astype(BF16)

    for c in range(chunks):
        columns = slice(c * chunk, (c + 1) * chunk)
        one_hot_lo(code[:, columns], hot_ref.at[:, columns])
        runs(c, 0.0, lhs_ref.at[c])
        lhs = lhs_ref[c]
        for at in range(c * chunk, (c + 1) * chunk, PIECE):
            choose(lhs, slice(at, at + PIECE), bin_row[:, at : at + PIECE], None)

    @pl.when(longest > LO)
    def _():
        passes = longest.astype(jnp.int32) // LO + 1

        def one_chunk(c, carry):
            def one_pass(k, carry):
                runs(c, (k * LO).astype(F32), lhs_ref.at[0])

                def one_piece(i, carry):
                    lanes = pl.ds(pl.multiple_of(c * chunk + i * PIECE, PIECE), PIECE)
                    part = code_ref[:, lanes]
                    now = part >> PLACE_BITS
                    turn = ((part & (2**PLACE_BITS - 1)) - bin_starts(start_ref[c], now)) >> LO_BITS
                    choose(lhs_ref[0], lanes, jnp.where(turn == k, now, -1), out_ref[:, lanes].astype(F32))
                    return carry

                return lax.fori_loop(0, chunk // PIECE, one_piece, carry)

            return lax.fori_loop(0, passes, one_pass, carry)

        lax.fori_loop(0, chunks, one_chunk, 0)


def restore(code, start, bins):
    slots, half_rows, bin_width = 2 * bins.shape[0], bins.shape[1], bins.shape[2] // 2
    width = code.shape[1]
    chunks = start.shape[0] - 1
    windows = -(-bin_width // LO)
    scratch = [
        pltpu.VMEM((windows, slots * half_rows, LO), F32),
        pltpu.VMEM((chunks, slots * half_rows, LO), BF16),
        pltpu.VMEM((LO, width), BF16),
    ]
    outs = [jax.ShapeDtypeStruct((2 * half_rows, width), BF16)]
    return on_core(restore_kernel, "restore", outs, [], [code, start, bins], 40, scratch)[0]


def partner(x):
    return lax.ppermute(x, "samples_2", [(0, 1), (1, 0)])


def exchange(x):
    return lax.all_to_all(x, CHIPS, split_axis=0, concat_axis=0, tiled=True)


def body(observed, labels, comp_sizes):
    row_local, width_local = observed.shape
    comps = comp_sizes.shape[0]
    groups = lax.axis_size("groups")
    row_count = row_local * lax.axis_size(SAMPLES)
    bin_width = 2 * width_local // comps
    slot = lax.axis_index(SAMPLES).astype(jnp.int32).reshape(1)
    message, code, start, places = partition(slot, comps, labels, observed)
    rows = exchange(message)
    square = jax.ShapeDtypeStruct((CMAX, CMAX), F32)
    powers = jax.ShapeDtypeStruct((3, CMAX, CMAX), F32)
    narrow = jax.ShapeDtypeStruct((CMAX, CMAX), BF16)
    pair = jax.ShapeDtypeStruct((2, CMAX, CMAX), BF16)
    tall = jax.ShapeDtypeStruct((row_count // 2, CMAX), BF16)
    flat = jax.ShapeDtypeStruct((row_count // 2, bin_width), BF16)
    small = jax.ShapeDtypeStruct((8, LANES), F32)
    back = jax.ShapeDtypeStruct((rows.shape[0], rows.shape[1], 2 * bin_width), BF16)
    gram, x, energy = on_core(
        gram_kernel, "gram", [square, tall, small], [slot], [places, rows, partner(rows)], 16
    )
    energies = [energy] + [
        lax.ppermute(energy, "groups", [(i, (i + k) % groups) for i in range(groups)]) for k in range(1, groups)
    ]
    build = functools.partial(powers_kernel, row_count=row_count)
    low, high, last, sums = on_core(build, "powers", [powers, powers, pair, small], [], [gram], 24)
    finish = functools.partial(inverse_kernel, entries=row_count * width_local * groups)
    (own,) = on_core(
        finish, "inverse", [narrow], [slot, comp_sizes], energies + [sums, low, high, last], 24
    )
    other = partner(own)
    done, waiting = on_core(whiten_own_kernel, "whiten_own", [flat, tall], [slot], [places, rows, x, own], 16)
    (mapped,) = on_core(
        whiten_other_kernel, "whiten_other", [back], [slot], [places, done, waiting, other], 16
    )
    return restore(code, start, exchange(mapped))


def solution(mesh):
    finer = Mesh(
        mesh.devices.reshape(8, 4, 2, mesh.shape["groups"]),
        ("samples_0", "samples_1", "samples_2", "groups"),
    )
    in_specs = (P(SAMPLES, "groups"), P("groups"), P("groups"))
    out_specs = P(SAMPLES, "groups")
    return jax.shard_map(body, mesh=finer, in_specs=in_specs, out_specs=out_specs, check_vma=False)
```

```python
import functools

import jax
import jax.numpy as jnp
from jax import lax
from jax.experimental import pallas as pl
from jax.experimental.pallas import tpu as pltpu
from jax.sharding import Mesh
from jax.sharding import PartitionSpec as P

CMAX = 512
ITERS = 5
LO = 256
LO_BITS = 8
PLACE_BITS = 10
LANES = 128
CHUNKS = 4
PIECE = 1024
CHIPS = ("samples_0", "samples_1")
SAMPLES = ("samples_0", "samples_1", "samples_2")
BF16 = jnp.bfloat16
F32 = jnp.float32

shrink = 0.2
ridge = 0.5


def iota(shape, axis):
    return lax.broadcasted_iota(jnp.int32, shape, axis)


def dot(a, b, contract=((1,), (0,))):
    return lax.dot_general(a, b, (contract, ((), ())), preferred_element_type=F32)


def halves(x):
    top = x.astype(BF16)
    return top, (x - top.astype(F32)).astype(BF16)


def one_hot_lo(place, ref):
    low = jnp.broadcast_to((place & (LO - 1)).astype(F32), (16, place.shape[1])).astype(BF16)
    level = iota((LO, LANES), 0).astype(F32).astype(BF16)
    for at in range(0, place.shape[1], LANES):
        lanes = slice(at, at + LANES)
        for r in range(0, LO, 16):
            same = level[r : r + 16] == low[:, lanes]
            ref[r : r + 16, lanes] = jnp.where(same, jnp.ones((16, LANES), BF16), jnp.zeros((16, LANES), BF16))


def window_of(begin):
    begin = jnp.concatenate([begin.astype(jnp.int32)] * (LO // LANES), axis=1)
    begin = jnp.broadcast_to(begin, (8, LO))
    return (begin >> LO_BITS) + jnp.where(iota((8, LO), 1) < (begin & (LO - 1)), 1, 0)


def bin_starts(start, bin_row):
    bins = start.shape[0]
    parts = []
    for at in range(0, bin_row.shape[1], LANES):
        same = iota((bins, LANES), 0) == bin_row[:, at : at + LANES]
        parts.append(jnp.sum(jnp.where(same, start, 0.0), axis=0, keepdims=True))
    return jnp.concatenate(parts, axis=1).astype(jnp.int32)


def places_kernel(labels_ref, code_ref, start_ref):
    width = labels_ref.shape[1]
    chunks, bins = start_ref.shape[0] - 1, start_ref.shape[1]
    chunk = width // chunks
    label = labels_ref[...] & (2 * bins - 1)
    bin_row = label >> 1
    upper = jnp.where(iota((LO, LO), 0) < iota((LO, LO), 1), 1.0, 0.0)
    counting = jnp.concatenate([upper, jnp.ones((LO, LANES), F32)], axis=1).astype(BF16)
    hots = [iota((bins, LO), 0) == bin_row[:, t : t + LO] for t in range(0, width, LO)]
    ones = jnp.concatenate([jnp.where(hot, 1.0, 0.0).astype(BF16) for hot in hots], axis=0)
    counts = dot(ones, counting)
    done = jnp.zeros((bins, LANES), F32)
    places = []
    for t, hot in enumerate(hots):
        if t * LO % chunk == 0:
            start_ref[t * LO // chunk] = done
        count = counts[t * bins : (t + 1) * bins]
        inside = jnp.concatenate([done] * (LO // LANES), axis=1) + count[:, :LO]
        places.append(jnp.sum(jnp.where(hot, inside, 0.0), axis=0, keepdims=True))
        done = done + count[:, LO:]
    start_ref[chunks] = done
    place = jnp.concatenate(places, axis=1).astype(jnp.int32)
    code_ref[...] = (label << PLACE_BITS) + place


def places_of(comps, labels, chunks=CHUNKS):
    width = labels.shape[0]
    outs = [
        jax.ShapeDtypeStruct((1, width), jnp.int32),
        jax.ShapeDtypeStruct((chunks + 1, comps // 2, LANES), F32),
    ]
    return on_core(places_kernel, "places", outs, [], [labels.reshape(1, width)], 16, work=2 * 10**9)


def longest_run(start_ref):
    most = start_ref[1] - start_ref[0]
    for c in range(1, start_ref.shape[0] - 1):
        most = jnp.maximum(most, start_ref[c + 1] - start_ref[c])
    return jnp.max(most)


def partition_kernel(slot_ref, code_ref, start_ref, x_ref, out_ref, own_ref, hot_ref, lhs_ref, acc_ref):
    rows, width = x_ref.shape
    chunks, bins = start_ref.shape[0] - 1, start_ref.shape[1]
    chunk = width // chunks
    windows = acc_ref.shape[0]
    bin_width = own_ref.shape[1]
    units = bin_width // LANES
    pair = slot_ref[0] // 2
    bin_row = code_ref[...] >> (PLACE_BITS + 1)
    place = code_ref[...] & (2**PLACE_BITS - 1)
    longest = longest_run(start_ref)

    def masked(c, bin_now, ref):
        columns = slice(c * chunk, (c + 1) * chunk)
        if not isinstance(c, int):
            columns = pl.ds(pl.multiple_of(c * chunk, chunk), chunk)
        x = x_ref[:, columns]
        bin_rows = jnp.broadcast_to(bin_now.astype(F32), (rows, chunk)).astype(BF16)
        for p in range(bins):
            ref[p * rows : (p + 1) * rows, :] = jnp.where(
                bin_rows == jnp.asarray(p, BF16), x, jnp.zeros_like(x)
            )
        mine = jnp.where(bin_now == pair, (code_ref[:, columns] >> PLACE_BITS) & 1, 0).astype(F32)
        ref[bins * rows :, :] = jnp.broadcast_to(mine, (rows, chunk)).astype(BF16)

    def first_places(c, p):
        if p < bins:
            return start_ref[c, p : p + 1, :]
        return start_ref[c, pl.ds(pair, 1), :]

    runs = []
    for c in range(chunks):
        columns = slice(c * chunk, (c + 1) * chunk)
        one_hot_lo(place[:, columns], hot_ref.at[c])
        masked(c, bin_row[:, columns], lhs_ref.at[c])
        runs.append(dot(lhs_ref[c], hot_ref[c], ((1,), (1,))))

    total = jnp.zeros((8, LANES), F32)
    for at in range(0, width, LANES):
        wide = x_ref[:, at : at + LANES].astype(F32)
        square = wide * wide
        for r in range(0, rows, 8):
            total = total + square[r : r + 8]
    total = whole(total, jnp.sum)
    first = total.astype(BF16).astype(F32)
    second = (total - first).astype(BF16).astype(F32)
    third = total - first - second
    row = iota((8, LANES), 0)
    pieces = jnp.where(row == 0, first, jnp.where(row == 1, second, jnp.where(row == 2, third, 0.0)))
    pieces = pieces.astype(BF16)

    for p in range(bins + 1):
        reached = [window_of(first_places(c, p)) for c in range(chunks)]
        for w in range(windows):
            hits = [window == w for window in reached]
            for half in range(2 if p < bins else 1):
                r = p * rows + half * 8
                value = jnp.where(hits[0], runs[0][r : r + 8], 0.0)
                for hit, run in zip(hits[1:], runs[1:]):
                    value = jnp.where(hit, run[r : r + 8], value)
                for side in range(LO // LANES):
                    u = w * (LO // LANES) + side
                    if u >= units:
                        continue
                    piece = value[:, side * LANES : (side + 1) * LANES]
                    if p < bins:
                        at = half * bin_width + u * LANES
                        out_ref[p, :, at : at + LANES] = piece.astype(BF16)
                    else:
                        own_ref[:, u * LANES : (u + 1) * LANES] = piece
    for p in range(bins):
        out_ref[p, :, 2 * bin_width :] = pieces

    @pl.when(longest > LO)
    def _():
        acc_ref[...] = jnp.zeros_like(acc_ref)
        passes = longest.astype(jnp.int32) // LO + 1

        def one_chunk(c, carry):
            code = code_ref[:, pl.ds(pl.multiple_of(c * chunk, chunk), chunk)]
            now = code >> (PLACE_BITS + 1)
            code = code & (2**PLACE_BITS - 1)
            turn = (code - bin_starts(start_ref[c], now)) >> LO_BITS

            def one_pass(k, carry):
                masked(c, jnp.where(turn == k, now, -1), lhs_ref.at[0])
                got = dot(lhs_ref[0], hot_ref[c], ((1,), (1,)))
                for p in range(bins + 1):
                    window = window_of(first_places(c, p) + (k * LO).astype(F32))
                    for w in range(windows):
                        for r in range(p * rows, (p + 1) * rows, 8):
                            acc_ref[w, r : r + 8] += jnp.where(window == w, got[r : r + 8], 0.0)
                return carry

            return lax.fori_loop(0, passes, one_pass, carry)

        lax.fori_loop(0, chunks, one_chunk, 0)
        for u in range(units):
            w, side = divmod(u, LO // LANES)
            lanes = slice(side * LANES, (side + 1) * LANES)
            own_ref[:, u * LANES : (u + 1) * LANES] = acc_ref[w, bins * rows : bins * rows + 8, lanes]
            for s in range(2 * bins):
                at = s % 2 * bin_width + u * LANES
                out_ref[s // 2, :, at : at + LANES] = acc_ref[w, s * 8 : s * 8 + 8, lanes].astype(BF16)

    below = jnp.where(iota((LANES, LANES), 0) < iota((LANES, LANES), 1), 1.0, 0.0)
    below = jnp.concatenate([below, jnp.ones((LANES, LANES), F32)], axis=1).astype(BF16)
    so_far = jnp.zeros((8, LANES), F32)
    row = iota((8, LANES), 0)
    for u in range(units):
        lanes = slice(u * LANES, (u + 1) * LANES)
        odds = own_ref[:, lanes]
        count = dot(odds.astype(BF16), below)
        place_odd = so_far + count[:, :LANES]
        place_even = (iota((8, LANES), 1) + u * LANES).astype(F32) - place_odd
        so_far = so_far + count[:, LANES:]
        own_ref[:, lanes] = jnp.where(
            row == 0, jnp.where(odds == 0.0, place_even, -1.0), jnp.where(odds == 1.0, place_odd, -1.0)
        )


def partition(slot, code, start, x):
    rows, width = x.shape
    chunks, bins = start.shape[0] - 1, start.shape[1]
    bin_width = width // bins
    windows = -(-bin_width // LO)
    chunk = width // chunks
    outs = [
        jax.ShapeDtypeStruct((bins, rows // 2, 2 * bin_width + LANES), BF16),
        jax.ShapeDtypeStruct((8, bin_width), F32),
        jax.ShapeDtypeStruct((chunks, LO, chunk), BF16),
    ]
    scratch = [
        pltpu.VMEM((chunks, (bins + 1) * rows, chunk), BF16),
        pltpu.VMEM((windows, (bins + 1) * rows, LO), F32),
    ]
    inputs = [code, start, x]
    return on_core(partition_kernel, "partition", outs, [slot], inputs, 38, scratch)


def product(a, b):
    return dot(a[0], b[0]) + (dot(a[0], b[1]) + dot(a[1], b[0]))


def whole(value, reduce):
    return reduce(reduce(value, axis=0, keepdims=True), axis=1, keepdims=True)


def compaction(places_ref, parity):
    place = places_ref[pl.ds(parity, 1), :].astype(jnp.int32)
    return jnp.where(iota((CMAX, places_ref.shape[1]), 0) == place, 1.0, 0.0).astype(BF16)


def groups_of_rows(ref, bin_width):
    for at in (0, bin_width):
        block = ref[:, :, at : at + bin_width]
        yield block.reshape(block.shape[0] * block.shape[1], bin_width)


def energy_of(ref, bin_width):
    return jnp.sum(ref[:, :, 2 * bin_width :].astype(F32), axis=0)


def gram_own_kernel(slot_ref, places_ref, rows_ref, gram_ref, x_ref, energy_ref):
    bin_width = places_ref.shape[1]
    pick = compaction(places_ref, slot_ref[0] % 2)
    at = 0
    for block in groups_of_rows(rows_ref, bin_width):
        x_ref[at : at + block.shape[0], :] = dot(block, pick, ((1,), (1,))).astype(BF16)
        at += block.shape[0]
    x = x_ref[...]
    gram_ref[...] = dot(x, x, ((0,), (0,)))
    energy_ref[...] = energy_of(rows_ref, bin_width)


def gram_other_kernel(slot_ref, places_ref, rows_ref, before_ref, energy_before_ref, gram_ref, energy_ref):
    bin_width = places_ref.shape[1]
    pick = compaction(places_ref, slot_ref[0] % 2)
    blocks = [dot(block, pick, ((1,), (1,))).astype(BF16) for block in groups_of_rows(rows_ref, bin_width)]
    x = jnp.concatenate(blocks, axis=0)
    gram_ref[...] = before_ref[...] + dot(x, x, ((0,), (0,)))
    energy_ref[...] = energy_before_ref[...] + energy_of(rows_ref, bin_width)


def powers_kernel(gram_ref, low_ref, high_ref, last_ref, sums_ref, *, row_count):
    covariance = gram_ref[...] * (1.0 / row_count)
    diagonal = iota((CMAX, CMAX), 0) == iota((CMAX, CMAX), 1)
    trace = whole(jnp.where(diagonal, covariance, 0.0), jnp.sum)
    shrunk = (1.0 - shrink) * covariance
    bound = whole(jnp.sum(jnp.abs(shrunk), axis=0, keepdims=True), jnp.max)
    base = jnp.where(diagonal, 1.0, 0.0) - shrunk * (1.0 / jnp.maximum(bound, 1e-30))
    row = iota((8, LANES), 0)
    sums_ref[...] = jnp.where(row == 0, trace, bound)
    for ref in (low_ref, high_ref):
        parts = halves(base)
        square = product(parts, parts)
        squares = halves(square)
        ref[0] = base
        ref[1] = square
        ref[2] = product(squares, parts)
        base = product(squares, squares)
    top, rest = halves(base)
    last_ref[0] = top
    last_ref[1] = rest


def inverse_kernel(slot_ref, sizes_ref, e0_ref, e1_ref, e2_ref, e3_ref, sums_ref, low_ref, high_ref, last_ref, out_ref, *, entries):
    size = sizes_ref[slot_ref[0]]
    energy = e0_ref[...] + e1_ref[...] + e2_ref[...] + e3_ref[...]
    average = (energy[0:1, :1] + energy[1:2, :1] + energy[2:3, :1]) * (1.0 / entries)
    trace, bound = sums_ref[0:1, :1], sums_ref[1:2, :1]
    lift = shrink * (trace / jnp.full((1, 1), size.astype(F32))) + ridge * average
    scale = 1.0 / (bound + lift)
    theta = bound * scale
    diagonal = jnp.where(iota((CMAX, CMAX), 0) == iota((CMAX, CMAX), 1), 1.0, 0.0)
    t2 = theta * theta
    t4 = t2 * t2
    t8 = t4 * t4
    low = diagonal + theta * low_ref[0] + t2 * low_ref[1] + (theta * t2) * low_ref[2]
    high = diagonal + t4 * high_ref[0] + t8 * high_ref[1] + (t4 * t8) * high_ref[2]
    total = product(halves(low), halves(high))
    total = total + (t8 * t8) * product(halves(total), (last_ref[0], last_ref[1]))
    out_ref[...] = (total * scale).astype(BF16)


def whiten_own_kernel(slot_ref, places_ref, rows_ref, x_ref, inverse_ref, done_ref, next_ref):
    parity = slot_ref[0] % 2
    bin_width = places_ref.shape[1]
    mapped = dot(x_ref[...], inverse_ref[...]).astype(BF16)
    done_ref[...] = dot(mapped, compaction(places_ref, parity)).astype(BF16)
    pick = compaction(places_ref, 1 - parity)
    at = 0
    for block in groups_of_rows(rows_ref, bin_width):
        next_ref[at : at + block.shape[0], :] = dot(block, pick, ((1,), (1,))).astype(BF16)
        at += block.shape[0]


def whiten_other_kernel(slot_ref, places_ref, done_ref, x_ref, inverse_ref, out_ref):
    pick = compaction(places_ref, 1 - slot_ref[0] % 2)
    mapped = dot(x_ref[...], inverse_ref[...]).astype(BF16)
    value = (done_ref[...].astype(F32) + dot(mapped, pick)).astype(BF16)
    count, bin_width = value.shape[0] // 2, value.shape[1]
    for half in range(2):
        block = value[half * count : (half + 1) * count].reshape(out_ref.shape[0], out_ref.shape[1], bin_width)
        out_ref[:, :, half * bin_width : (half + 1) * bin_width] = block


def on_core(kernel, name, outs, scalars, arrays, mebibytes, scratch=(), work=None):
    def spec(shape):
        return pl.BlockSpec(shape, lambda i: (0,) * len(shape))

    return pl.pallas_call(
        kernel,
        grid=(1,),
        in_specs=[pl.BlockSpec(memory_space=pltpu.SMEM) for _ in scalars] + [spec(a.shape) for a in arrays],
        out_specs=[spec(out.shape) for out in outs],
        out_shape=outs,
        scratch_shapes=list(scratch),
        compiler_params=pltpu.CompilerParams(vmem_limit_bytes=mebibytes << 20),
        cost_estimate=work and pl.CostEstimate(flops=work, bytes_accessed=1 << 17, transcendentals=0),
        name=name,
    )(*scalars, *arrays)


def restore_kernel(code_ref, start_ref, hot_ref, bins_ref, out_ref, mat_ref, lhs_ref):
    bins, half_rows, bin_width = bins_ref.shape
    bin_width = bin_width // 2
    rows, width = out_ref.shape
    slots = 2 * bins
    chunks = start_ref.shape[0] - 1
    chunk = width // chunks
    units = bin_width // LANES
    windows = mat_ref.shape[0]

    for w in range(windows):
        for side in range(LO // LANES):
            u = w * (LO // LANES) + side
            lanes = slice(side * LANES, (side + 1) * LANES)
            for s in range(slots):
                if u < units:
                    at = s % 2 * bin_width + u * LANES
                    piece = bins_ref[s // 2, :, at : at + LANES].astype(F32)
                else:
                    piece = jnp.zeros((half_rows, LANES), F32)
                mat_ref[w, s * half_rows : (s + 1) * half_rows, lanes] = piece
    code = code_ref[...]
    bin_row = code >> (PLACE_BITS + 1)
    longest = longest_run(start_ref)

    def runs(c, shift, ref):
        for p in range(bins):
            window = window_of(start_ref[c, p : p + 1, :] + shift)
            pieces = []
            for r in range(p * rows, (p + 1) * rows, 8):
                value = mat_ref[0, r : r + 8]
                for w in range(1, windows):
                    value = jnp.where(window == w, mat_ref[w, r : r + 8], value)
                pieces.append(value)
            ref[p * rows : (p + 1) * rows] = jnp.concatenate(pieces, axis=0).astype(BF16)

    def choose(lhs, hot, lanes, bin_now, old):
        got = dot(lhs, hot)
        bin_rows = jnp.broadcast_to(bin_now, (8, PIECE))
        for s in range(0, rows, 8):
            value = got[s : s + 8] if old is None else old[s : s + 8]
            for p in range(1 if old is None else 0, bins):
                value = jnp.where(bin_rows == p, got[p * rows + s : p * rows + s + 8], value)
            out_ref[s : s + 8, lanes] = value.astype(BF16)

    for c in range(chunks):
        runs(c, 0.0, lhs_ref.at[c])
        lhs = lhs_ref[c]
        for at in range(0, chunk, PIECE):
            lanes = slice(c * chunk + at, c * chunk + at + PIECE)
            choose(lhs, hot_ref[c, :, at : at + PIECE], lanes, bin_row[:, lanes], None)

    @pl.when(longest > LO)
    def _():
        passes = longest.astype(jnp.int32) // LO + 1

        def one_chunk(c, carry):
            def one_pass(k, carry):
                runs(c, (k * LO).astype(F32), lhs_ref.at[0])

                def one_piece(i, carry):
                    lanes = pl.ds(pl.multiple_of(c * chunk + i * PIECE, PIECE), PIECE)
                    part = code_ref[:, lanes]
                    now = part >> (PLACE_BITS + 1)
                    turn = ((part & (2**PLACE_BITS - 1)) - bin_starts(start_ref[c], now)) >> LO_BITS
                    hot = hot_ref[c, :, pl.ds(pl.multiple_of(i * PIECE, PIECE), PIECE)]
                    choose(lhs_ref[0], hot, lanes, jnp.where(turn == k, now, -1), out_ref[:, lanes].astype(F32))
                    return carry

                return lax.fori_loop(0, chunk // PIECE, one_piece, carry)

            return lax.fori_loop(0, passes, one_pass, carry)

        lax.fori_loop(0, chunks, one_chunk, 0)


def restore(code, start, hot, bins):
    slots, half_rows, bin_width = 2 * bins.shape[0], bins.shape[1], bins.shape[2] // 2
    width = code.shape[1]
    chunks = start.shape[0] - 1
    windows = -(-bin_width // LO)
    scratch = [
        pltpu.VMEM((windows, slots * half_rows, LO), F32),
        pltpu.VMEM((chunks, slots * half_rows, LO), BF16),
    ]
    outs = [jax.ShapeDtypeStruct((2 * half_rows, width), BF16)]
    return on_core(restore_kernel, "restore", outs, [], [code, start, hot, bins], 28, scratch)[0]


def partner(x):
    return lax.ppermute(x, "samples_2", [(0, 1), (1, 0)])


def exchange(x):
    return lax.all_to_all(x, CHIPS, split_axis=0, concat_axis=0, tiled=True)


def body(observed, labels, comp_sizes):
    row_local, width_local = observed.shape
    comps = comp_sizes.shape[0]
    groups = lax.axis_size("groups")
    row_count = row_local * lax.axis_size(SAMPLES)
    bin_width = 2 * width_local // comps
    slot = lax.axis_index(SAMPLES).astype(jnp.int32).reshape(1)
    code, start = places_of(comps, labels)
    message, places, hot = partition(slot, code, start, observed)
    rows = exchange(message)
    square = jax.ShapeDtypeStruct((CMAX, CMAX), F32)
    powers = jax.ShapeDtypeStruct((3, CMAX, CMAX), F32)
    narrow = jax.ShapeDtypeStruct((CMAX, CMAX), BF16)
    pair = jax.ShapeDtypeStruct((2, CMAX, CMAX), BF16)
    tall = jax.ShapeDtypeStruct((row_count // 2, CMAX), BF16)
    flat = jax.ShapeDtypeStruct((row_count // 2, bin_width), BF16)
    small = jax.ShapeDtypeStruct((8, LANES), F32)
    back = jax.ShapeDtypeStruct((rows.shape[0], rows.shape[1], 2 * bin_width), BF16)
    others = partner(rows)
    gram, x, energy = on_core(gram_own_kernel, "gram_own", [square, tall, small], [slot], [places, rows], 12)
    gram, energy = on_core(
        gram_other_kernel, "gram_other", [square, small], [slot], [places, others, gram, energy], 12
    )
    energies = [energy] + [
        lax.ppermute(energy, "groups", [(i, (i + k) % groups) for i in range(groups)]) for k in range(1, groups)
    ]
    build = functools.partial(powers_kernel, row_count=row_count)
    low, high, last, sums = on_core(build, "powers", [powers, powers, pair, small], [], [gram], 24)
    finish = functools.partial(inverse_kernel, entries=row_count * width_local * groups)
    (own,) = on_core(
        finish, "inverse", [narrow], [slot, comp_sizes], energies + [sums, low, high, last], 24
    )
    other = partner(own)
    done, waiting = on_core(whiten_own_kernel, "whiten_own", [flat, tall], [slot], [places, rows, x, own], 16)
    (mapped,) = on_core(
        whiten_other_kernel, "whiten_other", [back], [slot], [places, done, waiting, other], 16
    )
    return restore(code, start, hot, exchange(mapped))


def solution(mesh):
    finer = Mesh(
        mesh.devices.reshape(8, 4, 2, mesh.shape["groups"]),
        ("samples_0", "samples_1", "samples_2", "groups"),
    )
    in_specs = (P(SAMPLES, "groups"), P("groups"), P("groups"))
    out_specs = P(SAMPLES, "groups")
    return jax.shard_map(body, mesh=finer, in_specs=in_specs, out_specs=out_specs, check_vma=False)
```

```python
import functools

import jax
import jax.numpy as jnp
from jax import lax
from jax.experimental import pallas as pl
from jax.experimental.pallas import tpu as pltpu
from jax.sharding import Mesh
from jax.sharding import PartitionSpec as P

CMAX = 512
ITERS = 5
LO = 256
LO_BITS = 8
PLACE_BITS = 10
LANES = 128
CHUNKS = 4
PIECE = 1024
CHIPS = ("samples_0", "samples_1")
SAMPLES = ("samples_0", "samples_1", "samples_2")
BF16 = jnp.bfloat16
F32 = jnp.float32

shrink = 0.2
ridge = 0.5


def iota(shape, axis):
    return lax.broadcasted_iota(jnp.int32, shape, axis)


def dot(a, b, contract=((1,), (0,))):
    return lax.dot_general(a, b, (contract, ((), ())), preferred_element_type=F32)


def halves(x):
    top = x.astype(BF16)
    return top, (x - top.astype(F32)).astype(BF16)


def one_hot_lo(place, ref):
    low = jnp.broadcast_to((place & (LO - 1)).astype(F32), (16, place.shape[1])).astype(BF16)
    level = iota((LO, LANES), 0).astype(F32).astype(BF16)
    for at in range(0, place.shape[1], LANES):
        lanes = slice(at, at + LANES)
        for r in range(0, LO, 16):
            same = level[r : r + 16] == low[:, lanes]
            ref[r : r + 16, lanes] = jnp.where(same, jnp.ones((16, LANES), BF16), jnp.zeros((16, LANES), BF16))


def window_of(begin):
    begin = jnp.concatenate([begin.astype(jnp.int32)] * (LO // LANES), axis=1)
    begin = jnp.broadcast_to(begin, (8, LO))
    return (begin >> LO_BITS) + jnp.where(iota((8, LO), 1) < (begin & (LO - 1)), 1, 0)


def bin_starts(start, bin_row):
    bins = start.shape[0]
    parts = []
    for at in range(0, bin_row.shape[1], LANES):
        same = iota((bins, LANES), 0) == bin_row[:, at : at + LANES]
        parts.append(jnp.sum(jnp.where(same, start, 0.0), axis=0, keepdims=True))
    return jnp.concatenate(parts, axis=1).astype(jnp.int32)


def places_kernel(labels_ref, code_ref, start_ref):
    width = labels_ref.shape[1]
    chunks, bins = start_ref.shape[0] - 1, start_ref.shape[1]
    chunk = width // chunks
    label = labels_ref[...] & (2 * bins - 1)
    bin_row = label >> 1
    upper = jnp.where(iota((LO, LO), 0) < iota((LO, LO), 1), 1.0, 0.0)
    counting = jnp.concatenate([upper, jnp.ones((LO, LANES), F32)], axis=1).astype(BF16)
    hots = [iota((bins, LO), 0) == bin_row[:, t : t + LO] for t in range(0, width, LO)]
    ones = jnp.concatenate([jnp.where(hot, 1.0, 0.0).astype(BF16) for hot in hots], axis=0)
    counts = dot(ones, counting)
    done = jnp.zeros((bins, LANES), F32)
    places = []
    for t, hot in enumerate(hots):
        if t * LO % chunk == 0:
            start_ref[t * LO // chunk] = done
        count = counts[t * bins : (t + 1) * bins]
        inside = jnp.concatenate([done] * (LO // LANES), axis=1) + count[:, :LO]
        places.append(jnp.sum(jnp.where(hot, inside, 0.0), axis=0, keepdims=True))
        done = done + count[:, LO:]
    start_ref[chunks] = done
    place = jnp.concatenate(places, axis=1).astype(jnp.int32)
    code_ref[...] = (label << PLACE_BITS) + place


def places_of(comps, labels, chunks=CHUNKS):
    width = labels.shape[0]
    outs = [
        jax.ShapeDtypeStruct((1, width), jnp.int32),
        jax.ShapeDtypeStruct((chunks + 1, comps // 2, LANES), F32),
    ]
    return on_core(places_kernel, "places", outs, [], [labels.reshape(1, width)], 16, work=8 * 10**9)


def longest_run(start_ref):
    most = start_ref[1] - start_ref[0]
    for c in range(1, start_ref.shape[0] - 1):
        most = jnp.maximum(most, start_ref[c + 1] - start_ref[c])
    return jnp.max(most)


def partition_kernel(slot_ref, code_ref, start_ref, x_ref, out_ref, own_ref, hot_ref, lhs_ref, acc_ref):
    rows, width = x_ref.shape
    chunks, bins = start_ref.shape[0] - 1, start_ref.shape[1]
    chunk = width // chunks
    windows = acc_ref.shape[0]
    bin_width = own_ref.shape[1]
    units = bin_width // LANES
    pair = slot_ref[0] // 2
    bin_row = code_ref[...] >> (PLACE_BITS + 1)
    place = code_ref[...] & (2**PLACE_BITS - 1)
    longest = longest_run(start_ref)

    def masked(c, bin_now, ref):
        columns = slice(c * chunk, (c + 1) * chunk)
        if not isinstance(c, int):
            columns = pl.ds(pl.multiple_of(c * chunk, chunk), chunk)
        x = x_ref[:, columns]
        bin_rows = jnp.broadcast_to(bin_now.astype(F32), (rows, chunk)).astype(BF16)
        for p in range(bins):
            ref[p * rows : (p + 1) * rows, :] = jnp.where(
                bin_rows == jnp.asarray(p, BF16), x, jnp.zeros_like(x)
            )
        mine = jnp.where(bin_now == pair, (code_ref[:, columns] >> PLACE_BITS) & 1, 0).astype(F32)
        ref[bins * rows :, :] = jnp.broadcast_to(mine, (rows, chunk)).astype(BF16)

    def first_places(c, p):
        if p < bins:
            return start_ref[c, p : p + 1, :]
        return start_ref[c, pl.ds(pair, 1), :]

    runs = []
    for c in range(chunks):
        columns = slice(c * chunk, (c + 1) * chunk)
        one_hot_lo(place[:, columns], hot_ref.at[c])
        masked(c, bin_row[:, columns], lhs_ref.at[c])
        runs.append(dot(lhs_ref[c], hot_ref[c], ((1,), (1,))))

    total = jnp.zeros((8, LANES), F32)
    for at in range(0, width, LANES):
        wide = x_ref[:, at : at + LANES].astype(F32)
        square = wide * wide
        for r in range(0, rows, 8):
            total = total + square[r : r + 8]
    total = whole(total, jnp.sum)
    first = total.astype(BF16).astype(F32)
    second = (total - first).astype(BF16).astype(F32)
    third = total - first - second
    row = iota((8, LANES), 0)
    pieces = jnp.where(row == 0, first, jnp.where(row == 1, second, jnp.where(row == 2, third, 0.0)))
    pieces = pieces.astype(BF16)

    for p in range(bins + 1):
        reached = [window_of(first_places(c, p)) for c in range(chunks)]
        for w in range(windows):
            hits = [window == w for window in reached]
            for half in range(2 if p < bins else 1):
                r = p * rows + half * 8
                value = jnp.where(hits[0], runs[0][r : r + 8], 0.0)
                for hit, run in zip(hits[1:], runs[1:]):
                    value = jnp.where(hit, run[r : r + 8], value)
                for side in range(LO // LANES):
                    u = w * (LO // LANES) + side
                    if u >= units:
                        continue
                    piece = value[:, side * LANES : (side + 1) * LANES]
                    if p < bins:
                        at = half * bin_width + u * LANES
                        out_ref[p, :, at : at + LANES] = piece.astype(BF16)
                    else:
                        own_ref[:, u * LANES : (u + 1) * LANES] = piece
    for p in range(bins):
        out_ref[p, :, 2 * bin_width :] = pieces

    @pl.when(longest > LO)
    def _():
        acc_ref[...] = jnp.zeros_like(acc_ref)
        passes = longest.astype(jnp.int32) // LO + 1

        def one_chunk(c, carry):
            code = code_ref[:, pl.ds(pl.multiple_of(c * chunk, chunk), chunk)]
            now = code >> (PLACE_BITS + 1)
            code = code & (2**PLACE_BITS - 1)
            turn = (code - bin_starts(start_ref[c], now)) >> LO_BITS

            def one_pass(k, carry):
                masked(c, jnp.where(turn == k, now, -1), lhs_ref.at[0])
                got = dot(lhs_ref[0], hot_ref[c], ((1,), (1,)))
                for p in range(bins + 1):
                    window = window_of(first_places(c, p) + (k * LO).astype(F32))
                    for w in range(windows):
                        for r in range(p * rows, (p + 1) * rows, 8):
                            acc_ref[w, r : r + 8] += jnp.where(window == w, got[r : r + 8], 0.0)
                return carry

            return lax.fori_loop(0, passes, one_pass, carry)

        lax.fori_loop(0, chunks, one_chunk, 0)
        for u in range(units):
            w, side = divmod(u, LO // LANES)
            lanes = slice(side * LANES, (side + 1) * LANES)
            own_ref[:, u * LANES : (u + 1) * LANES] = acc_ref[w, bins * rows : bins * rows + 8, lanes]
            for s in range(2 * bins):
                at = s % 2 * bin_width + u * LANES
                out_ref[s // 2, :, at : at + LANES] = acc_ref[w, s * 8 : s * 8 + 8, lanes].astype(BF16)

    below = jnp.where(iota((LANES, LANES), 0) < iota((LANES, LANES), 1), 1.0, 0.0)
    below = jnp.concatenate([below, jnp.ones((LANES, LANES), F32)], axis=1).astype(BF16)
    so_far = jnp.zeros((8, LANES), F32)
    row = iota((8, LANES), 0)
    for u in range(units):
        lanes = slice(u * LANES, (u + 1) * LANES)
        odds = own_ref[:, lanes]
        count = dot(odds.astype(BF16), below)
        place_odd = so_far + count[:, :LANES]
        place_even = (iota((8, LANES), 1) + u * LANES).astype(F32) - place_odd
        so_far = so_far + count[:, LANES:]
        own_ref[:, lanes] = jnp.where(
            row == 0, jnp.where(odds == 0.0, place_even, -1.0), jnp.where(odds == 1.0, place_odd, -1.0)
        )


def partition(slot, code, start, x):
    rows, width = x.shape
    chunks, bins = start.shape[0] - 1, start.shape[1]
    bin_width = width // bins
    windows = -(-bin_width // LO)
    chunk = width // chunks
    outs = [
        jax.ShapeDtypeStruct((bins, rows // 2, 2 * bin_width + LANES), BF16),
        jax.ShapeDtypeStruct((8, bin_width), F32),
        jax.ShapeDtypeStruct((chunks, LO, chunk), BF16),
    ]
    scratch = [
        pltpu.VMEM((chunks, (bins + 1) * rows, chunk), BF16),
        pltpu.VMEM((windows, (bins + 1) * rows, LO), F32),
    ]
    inputs = [code, start, x]
    return on_core(partition_kernel, "partition", outs, [slot], inputs, 38, scratch)


def product(a, b):
    return dot(a[0], b[0]) + (dot(a[0], b[1]) + dot(a[1], b[0]))


def whole(value, reduce):
    return reduce(reduce(value, axis=0, keepdims=True), axis=1, keepdims=True)


def compaction(places_ref, parity):
    place = places_ref[pl.ds(parity, 1), :].astype(jnp.int32)
    return jnp.where(iota((CMAX, places_ref.shape[1]), 0) == place, 1.0, 0.0).astype(BF16)


def groups_of_rows(ref, bin_width):
    for at in (0, bin_width):
        block = ref[:, :, at : at + bin_width]
        yield block.reshape(block.shape[0] * block.shape[1], bin_width)


def energy_of(ref, bin_width):
    return jnp.sum(ref[:, :, 2 * bin_width :].astype(F32), axis=0)


def gram_own_kernel(slot_ref, places_ref, rows_ref, gram_ref, x_ref, energy_ref):
    bin_width = places_ref.shape[1]
    pick = compaction(places_ref, slot_ref[0] % 2)
    at = 0
    for block in groups_of_rows(rows_ref, bin_width):
        x_ref[at : at + block.shape[0], :] = dot(block, pick, ((1,), (1,))).astype(BF16)
        at += block.shape[0]
    x = x_ref[...]
    gram_ref[...] = dot(x, x, ((0,), (0,)))
    energy_ref[...] = energy_of(rows_ref, bin_width)


def gram_other_kernel(slot_ref, places_ref, rows_ref, before_ref, energy_before_ref, gram_ref, energy_ref):
    bin_width = places_ref.shape[1]
    pick = compaction(places_ref, slot_ref[0] % 2)
    blocks = [dot(block, pick, ((1,), (1,))).astype(BF16) for block in groups_of_rows(rows_ref, bin_width)]
    x = jnp.concatenate(blocks, axis=0)
    gram_ref[...] = before_ref[...] + dot(x, x, ((0,), (0,)))
    energy_ref[...] = energy_before_ref[...] + energy_of(rows_ref, bin_width)


def first_powers_kernel(gram_ref, low_ref, fourth_ref, sums_ref, *, row_count):
    covariance = gram_ref[...] * (1.0 / row_count)
    diagonal = iota((CMAX, CMAX), 0) == iota((CMAX, CMAX), 1)
    trace = whole(jnp.where(diagonal, covariance, 0.0), jnp.sum)
    shrunk = (1.0 - shrink) * covariance
    bound = whole(jnp.sum(jnp.abs(shrunk), axis=0, keepdims=True), jnp.max)
    base = jnp.where(diagonal, 1.0, 0.0) - shrunk * (1.0 / jnp.maximum(bound, 1e-30))
    row = iota((8, LANES), 0)
    sums_ref[...] = jnp.where(row == 0, trace, bound)
    parts = halves(base)
    square = product(parts, parts)
    squares = halves(square)
    low_ref[0] = base
    low_ref[1] = square
    low_ref[2] = product(squares, parts)
    fourth_ref[...] = product(squares, squares)


def eighth_power_kernel(fourth_ref, energy_ref, neighbour_ref, eighth_ref, sum_ref):
    parts = halves(fourth_ref[...])
    eighth_ref[...] = product(parts, parts)
    sum_ref[...] = energy_ref[...] + neighbour_ref[...]


def last_powers_kernel(fourth_ref, eighth_ref, twelfth_ref, last_ref):
    parts = halves(eighth_ref[...])
    twelfth_ref[...] = product(parts, halves(fourth_ref[...]))
    top, rest = halves(product(parts, parts))
    last_ref[0] = top
    last_ref[1] = rest


def inverse_kernel(
    slot_ref, sizes_ref, e0_ref, e1_ref, sums_ref, low_ref, fourth_ref, eighth_ref, twelfth_ref, last_ref, out_ref, *, entries
):
    size = sizes_ref[slot_ref[0]]
    energy = e0_ref[...] + e1_ref[...]
    average = (energy[0:1, :1] + energy[1:2, :1] + energy[2:3, :1]) * (1.0 / entries)
    trace, bound = sums_ref[0:1, :1], sums_ref[1:2, :1]
    lift = shrink * (trace / jnp.full((1, 1), size.astype(F32))) + ridge * average
    scale = 1.0 / (bound + lift)
    theta = bound * scale
    diagonal = jnp.where(iota((CMAX, CMAX), 0) == iota((CMAX, CMAX), 1), 1.0, 0.0)
    t2 = theta * theta
    t4 = t2 * t2
    t8 = t4 * t4
    low = diagonal + theta * low_ref[0] + t2 * low_ref[1] + (theta * t2) * low_ref[2]
    high = diagonal + t4 * fourth_ref[...] + t8 * eighth_ref[...] + (t4 * t8) * twelfth_ref[...]
    total = product(halves(low), halves(high))
    total = total + (t8 * t8) * product(halves(total), (last_ref[0], last_ref[1]))
    out_ref[...] = (total * scale).astype(BF16)


def whiten_own_kernel(slot_ref, places_ref, rows_ref, x_ref, inverse_ref, done_ref, next_ref):
    parity = slot_ref[0] % 2
    bin_width = places_ref.shape[1]
    mapped = dot(x_ref[...], inverse_ref[...]).astype(BF16)
    done_ref[...] = dot(mapped, compaction(places_ref, parity)).astype(BF16)
    pick = compaction(places_ref, 1 - parity)
    at = 0
    for block in groups_of_rows(rows_ref, bin_width):
        next_ref[at : at + block.shape[0], :] = dot(block, pick, ((1,), (1,))).astype(BF16)
        at += block.shape[0]


def whiten_other_kernel(slot_ref, places_ref, done_ref, x_ref, inverse_ref, out_ref):
    pick = compaction(places_ref, 1 - slot_ref[0] % 2)
    mapped = dot(x_ref[...], inverse_ref[...]).astype(BF16)
    value = (done_ref[...].astype(F32) + dot(mapped, pick)).astype(BF16)
    count, bin_width = value.shape[0] // 2, value.shape[1]
    for half in range(2):
        block = value[half * count : (half + 1) * count].reshape(out_ref.shape[0], out_ref.shape[1], bin_width)
        out_ref[:, :, half * bin_width : (half + 1) * bin_width] = block


def on_core(kernel, name, outs, scalars, arrays, mebibytes, scratch=(), work=None):
    def spec(shape):
        return pl.BlockSpec(shape, lambda i: (0,) * len(shape))

    return pl.pallas_call(
        kernel,
        grid=(1,),
        in_specs=[pl.BlockSpec(memory_space=pltpu.SMEM) for _ in scalars] + [spec(a.shape) for a in arrays],
        out_specs=[spec(out.shape) for out in outs],
        out_shape=outs,
        scratch_shapes=list(scratch),
        compiler_params=pltpu.CompilerParams(vmem_limit_bytes=mebibytes << 20),
        cost_estimate=work and pl.CostEstimate(flops=work, bytes_accessed=1 << 17, transcendentals=0),
        name=name,
    )(*scalars, *arrays)


def restore_kernel(code_ref, start_ref, hot_ref, bins_ref, out_ref, mat_ref, lhs_ref):
    bins, half_rows, bin_width = bins_ref.shape
    bin_width = bin_width // 2
    rows, width = out_ref.shape
    slots = 2 * bins
    chunks = start_ref.shape[0] - 1
    chunk = width // chunks
    units = bin_width // LANES
    windows = mat_ref.shape[0]

    for w in range(windows):
        for side in range(LO // LANES):
            u = w * (LO // LANES) + side
            lanes = slice(side * LANES, (side + 1) * LANES)
            for s in range(slots):
                if u < units:
                    at = s % 2 * bin_width + u * LANES
                    piece = bins_ref[s // 2, :, at : at + LANES].astype(F32)
                else:
                    piece = jnp.zeros((half_rows, LANES), F32)
                mat_ref[w, s * half_rows : (s + 1) * half_rows, lanes] = piece
    code = code_ref[...]
    bin_row = code >> (PLACE_BITS + 1)
    longest = longest_run(start_ref)

    def runs(c, shift, ref):
        for p in range(bins):
            window = window_of(start_ref[c, p : p + 1, :] + shift)
            pieces = []
            for r in range(p * rows, (p + 1) * rows, 8):
                value = mat_ref[0, r : r + 8]
                for w in range(1, windows):
                    value = jnp.where(window == w, mat_ref[w, r : r + 8], value)
                pieces.append(value)
            ref[p * rows : (p + 1) * rows] = jnp.concatenate(pieces, axis=0).astype(BF16)

    def choose(lhs, hot, lanes, bin_now, old):
        got = dot(lhs, hot)
        bin_rows = jnp.broadcast_to(bin_now, (8, PIECE))
        for s in range(0, rows, 8):
            value = got[s : s + 8] if old is None else old[s : s + 8]
            for p in range(1 if old is None else 0, bins):
                value = jnp.where(bin_rows == p, got[p * rows + s : p * rows + s + 8], value)
            out_ref[s : s + 8, lanes] = value.astype(BF16)

    for c in range(chunks):
        runs(c, 0.0, lhs_ref.at[c])
        lhs = lhs_ref[c]
        for at in range(0, chunk, PIECE):
            lanes = slice(c * chunk + at, c * chunk + at + PIECE)
            choose(lhs, hot_ref[c, :, at : at + PIECE], lanes, bin_row[:, lanes], None)

    @pl.when(longest > LO)
    def _():
        passes = longest.astype(jnp.int32) // LO + 1

        def one_chunk(c, carry):
            def one_pass(k, carry):
                runs(c, (k * LO).astype(F32), lhs_ref.at[0])

                def one_piece(i, carry):
                    lanes = pl.ds(pl.multiple_of(c * chunk + i * PIECE, PIECE), PIECE)
                    part = code_ref[:, lanes]
                    now = part >> (PLACE_BITS + 1)
                    turn = ((part & (2**PLACE_BITS - 1)) - bin_starts(start_ref[c], now)) >> LO_BITS
                    hot = hot_ref[c, :, pl.ds(pl.multiple_of(i * PIECE, PIECE), PIECE)]
                    choose(lhs_ref[0], hot, lanes, jnp.where(turn == k, now, -1), out_ref[:, lanes].astype(F32))
                    return carry

                return lax.fori_loop(0, chunk // PIECE, one_piece, carry)

            return lax.fori_loop(0, passes, one_pass, carry)

        lax.fori_loop(0, chunks, one_chunk, 0)


def restore(code, start, hot, bins):
    slots, half_rows, bin_width = 2 * bins.shape[0], bins.shape[1], bins.shape[2] // 2
    width = code.shape[1]
    chunks = start.shape[0] - 1
    windows = -(-bin_width // LO)
    scratch = [
        pltpu.VMEM((windows, slots * half_rows, LO), F32),
        pltpu.VMEM((chunks, slots * half_rows, LO), BF16),
    ]
    outs = [jax.ShapeDtypeStruct((2 * half_rows, width), BF16)]
    return on_core(restore_kernel, "restore", outs, [], [code, start, hot, bins], 28, scratch)[0]


def partner(x):
    return lax.ppermute(x, "samples_2", [(0, 1), (1, 0)])


def across(x, apart):
    return lax.ppermute(x, "groups", [(i, i ^ apart) for i in range(lax.axis_size("groups"))])


def exchange(x):
    return lax.all_to_all(x, CHIPS, split_axis=0, concat_axis=0, tiled=True)


def body(observed, labels, comp_sizes):
    row_local, width_local = observed.shape
    comps = comp_sizes.shape[0]
    groups = lax.axis_size("groups")
    row_count = row_local * lax.axis_size(SAMPLES)
    bin_width = 2 * width_local // comps
    slot = lax.axis_index(SAMPLES).astype(jnp.int32).reshape(1)
    code, start = places_of(comps, labels)
    message, places, hot = partition(slot, code, start, observed)
    rows = exchange(message)
    square = jax.ShapeDtypeStruct((CMAX, CMAX), F32)
    powers = jax.ShapeDtypeStruct((3, CMAX, CMAX), F32)
    narrow = jax.ShapeDtypeStruct((CMAX, CMAX), BF16)
    pair = jax.ShapeDtypeStruct((2, CMAX, CMAX), BF16)
    tall = jax.ShapeDtypeStruct((row_count // 2, CMAX), BF16)
    flat = jax.ShapeDtypeStruct((row_count // 2, bin_width), BF16)
    small = jax.ShapeDtypeStruct((8, LANES), F32)
    back = jax.ShapeDtypeStruct((rows.shape[0], rows.shape[1], 2 * bin_width), BF16)
    others = partner(rows)
    gram, x, energy = on_core(gram_own_kernel, "gram_own", [square, tall, small], [slot], [places, rows], 12)
    gram, energy = on_core(
        gram_other_kernel, "gram_other", [square, small], [slot], [places, others, gram, energy], 12
    )
    neighbour = across(energy, 1)
    build = functools.partial(first_powers_kernel, row_count=row_count)
    low, fourth, sums = on_core(build, "first_powers", [powers, square, small], [], [gram], 16)
    eighth, energy = on_core(
        eighth_power_kernel, "eighth_power", [square, small], [], [fourth, energy, neighbour], 12
    )
    others = across(energy, 2)
    twelfth, last = on_core(last_powers_kernel, "last_powers", [square, pair], [], [fourth, eighth], 16)
    finish = functools.partial(inverse_kernel, entries=row_count * width_local * groups)
    (own,) = on_core(
        finish,
        "inverse",
        [narrow],
        [slot, comp_sizes],
        [energy, others, sums, low, fourth, eighth, twelfth, last],
        24,
    )
    other = partner(own)
    done, waiting = on_core(whiten_own_kernel, "whiten_own", [flat, tall], [slot], [places, rows, x, own], 16)
    (mapped,) = on_core(
        whiten_other_kernel, "whiten_other", [back], [slot], [places, done, waiting, other], 16
    )
    return restore(code, start, hot, exchange(mapped))


def solution(mesh):
    finer = Mesh(
        mesh.devices.reshape(8, 4, 2, mesh.shape["groups"]),
        ("samples_0", "samples_1", "samples_2", "groups"),
    )
    in_specs = (P(SAMPLES, "groups"), P("groups"), P("groups"))
    out_specs = P(SAMPLES, "groups")
    return jax.shard_map(body, mesh=finer, in_specs=in_specs, out_specs=out_specs, check_vma=False)
```

```python
import functools

import jax
import jax.numpy as jnp
from jax import lax
from jax.experimental import pallas as pl
from jax.experimental.pallas import tpu as pltpu
from jax.sharding import Mesh
from jax.sharding import PartitionSpec as P

CMAX = 512
ITERS = 5
LO = 256
LO_BITS = 8
PLACE_BITS = 10
LANES = 128
CHUNKS = 4
PIECE = 1024
CHIPS = ("samples_0", "samples_1")
SAMPLES = ("samples_0", "samples_1", "samples_2")
BF16 = jnp.bfloat16
F32 = jnp.float32

shrink = 0.2
ridge = 0.5


def iota(shape, axis):
    return lax.broadcasted_iota(jnp.int32, shape, axis)


def dot(a, b, contract=((1,), (0,))):
    return lax.dot_general(a, b, (contract, ((), ())), preferred_element_type=F32)


def halves(x):
    top = x.astype(BF16)
    return top, (x - top.astype(F32)).astype(BF16)


def one_hot_lo(place, ref):
    low = jnp.broadcast_to((place & (LO - 1)).astype(F32), (16, place.shape[1])).astype(BF16)
    level = iota((LO, LANES), 0).astype(F32).astype(BF16)
    for at in range(0, place.shape[1], LANES):
        lanes = slice(at, at + LANES)
        for r in range(0, LO, 16):
            same = level[r : r + 16] == low[:, lanes]
            ref[r : r + 16, lanes] = jnp.where(same, jnp.ones((16, LANES), BF16), jnp.zeros((16, LANES), BF16))


def window_of(begin):
    begin = jnp.concatenate([begin.astype(jnp.int32)] * (LO // LANES), axis=1)
    begin = jnp.broadcast_to(begin, (8, LO))
    return (begin >> LO_BITS) + jnp.where(iota((8, LO), 1) < (begin & (LO - 1)), 1, 0)


def bin_starts(start, bin_row):
    bins = start.shape[0]
    parts = []
    for at in range(0, bin_row.shape[1], LANES):
        same = iota((bins, LANES), 0) == bin_row[:, at : at + LANES]
        parts.append(jnp.sum(jnp.where(same, start, 0.0), axis=0, keepdims=True))
    return jnp.concatenate(parts, axis=1).astype(jnp.int32)


def places_kernel(labels_ref, code_ref, start_ref):
    width = labels_ref.shape[1]
    chunks, bins = start_ref.shape[0] - 1, start_ref.shape[1]
    chunk = width // chunks
    label = labels_ref[...] & (2 * bins - 1)
    bin_row = label >> 1
    upper = jnp.where(iota((LO, LO), 0) < iota((LO, LO), 1), 1.0, 0.0)
    counting = jnp.concatenate([upper, jnp.ones((LO, LANES), F32)], axis=1).astype(BF16)
    hots = [iota((bins, LO), 0) == bin_row[:, t : t + LO] for t in range(0, width, LO)]
    ones = jnp.concatenate([jnp.where(hot, 1.0, 0.0).astype(BF16) for hot in hots], axis=0)
    counts = dot(ones, counting)
    done = jnp.zeros((bins, LANES), F32)
    places = []
    for t, hot in enumerate(hots):
        if t * LO % chunk == 0:
            start_ref[t * LO // chunk] = done
        count = counts[t * bins : (t + 1) * bins]
        inside = jnp.concatenate([done] * (LO // LANES), axis=1) + count[:, :LO]
        places.append(jnp.sum(jnp.where(hot, inside, 0.0), axis=0, keepdims=True))
        done = done + count[:, LO:]
    start_ref[chunks] = done
    place = jnp.concatenate(places, axis=1).astype(jnp.int32)
    code_ref[...] = (label << PLACE_BITS) + place


def places_of(comps, labels, chunks=CHUNKS):
    width = labels.shape[0]
    outs = [
        jax.ShapeDtypeStruct((1, width), jnp.int32),
        jax.ShapeDtypeStruct((chunks + 1, comps // 2, LANES), F32),
    ]
    return on_core(places_kernel, "places", outs, [], [labels.reshape(1, width)], 16, work=8 * 10**9)


def longest_run(start_ref):
    most = start_ref[1] - start_ref[0]
    for c in range(1, start_ref.shape[0] - 1):
        most = jnp.maximum(most, start_ref[c + 1] - start_ref[c])
    return jnp.max(most)


def partition_kernel(slot_ref, code_ref, start_ref, x_ref, out_ref, own_ref, hot_ref, lhs_ref, acc_ref):
    rows, width = x_ref.shape
    chunks, bins = start_ref.shape[0] - 1, start_ref.shape[1]
    chunk = width // chunks
    windows = acc_ref.shape[0]
    bin_width = own_ref.shape[1]
    units = bin_width // LANES
    pair = slot_ref[0] // 2
    bin_row = code_ref[...] >> (PLACE_BITS + 1)
    place = code_ref[...] & (2**PLACE_BITS - 1)
    longest = longest_run(start_ref)

    def masked(c, bin_now, ref):
        columns = slice(c * chunk, (c + 1) * chunk)
        if not isinstance(c, int):
            columns = pl.ds(pl.multiple_of(c * chunk, chunk), chunk)
        x = x_ref[:, columns]
        bin_rows = jnp.broadcast_to(bin_now.astype(F32), (rows, chunk)).astype(BF16)
        for p in range(bins):
            ref[p * rows : (p + 1) * rows, :] = jnp.where(
                bin_rows == jnp.asarray(p, BF16), x, jnp.zeros_like(x)
            )
        mine = jnp.where(bin_now == pair, (code_ref[:, columns] >> PLACE_BITS) & 1, 0).astype(F32)
        ref[bins * rows :, :] = jnp.broadcast_to(mine, (rows, chunk)).astype(BF16)

    def first_places(c, p):
        if p < bins:
            return start_ref[c, p : p + 1, :]
        return start_ref[c, pl.ds(pair, 1), :]

    runs = []
    for c in range(chunks):
        columns = slice(c * chunk, (c + 1) * chunk)
        one_hot_lo(place[:, columns], hot_ref.at[c])
        masked(c, bin_row[:, columns], lhs_ref.at[c])
        runs.append(dot(lhs_ref[c], hot_ref[c], ((1,), (1,))))

    total = jnp.zeros((8, LANES), F32)
    for at in range(0, width, LANES):
        wide = x_ref[:, at : at + LANES].astype(F32)
        square = wide * wide
        for r in range(0, rows, 8):
            total = total + square[r : r + 8]
    total = whole(total, jnp.sum)
    first = total.astype(BF16).astype(F32)
    second = (total - first).astype(BF16).astype(F32)
    third = total - first - second
    row = iota((8, LANES), 0)
    pieces = jnp.where(row == 0, first, jnp.where(row == 1, second, jnp.where(row == 2, third, 0.0)))
    pieces = pieces.astype(BF16)

    for p in range(bins + 1):
        reached = [window_of(first_places(c, p)) for c in range(chunks)]
        for w in range(windows):
            hits = [window == w for window in reached]
            for half in range(2 if p < bins else 1):
                r = p * rows + half * 8
                value = jnp.where(hits[0], runs[0][r : r + 8], 0.0)
                for hit, run in zip(hits[1:], runs[1:]):
                    value = jnp.where(hit, run[r : r + 8], value)
                for side in range(LO // LANES):
                    u = w * (LO // LANES) + side
                    if u >= units:
                        continue
                    piece = value[:, side * LANES : (side + 1) * LANES]
                    if p < bins:
                        at = half * bin_width + u * LANES
                        out_ref[p, :, at : at + LANES] = piece.astype(BF16)
                    else:
                        own_ref[:, u * LANES : (u + 1) * LANES] = piece
    for p in range(bins):
        out_ref[p, :, 2 * bin_width :] = pieces

    @pl.when(longest > LO)
    def _():
        acc_ref[...] = jnp.zeros_like(acc_ref)
        passes = longest.astype(jnp.int32) // LO + 1

        def one_chunk(c, carry):
            code = code_ref[:, pl.ds(pl.multiple_of(c * chunk, chunk), chunk)]
            now = code >> (PLACE_BITS + 1)
            code = code & (2**PLACE_BITS - 1)
            turn = (code - bin_starts(start_ref[c], now)) >> LO_BITS

            def one_pass(k, carry):
                masked(c, jnp.where(turn == k, now, -1), lhs_ref.at[0])
                got = dot(lhs_ref[0], hot_ref[c], ((1,), (1,)))
                for p in range(bins + 1):
                    window = window_of(first_places(c, p) + (k * LO).astype(F32))
                    for w in range(windows):
                        for r in range(p * rows, (p + 1) * rows, 8):
                            acc_ref[w, r : r + 8] += jnp.where(window == w, got[r : r + 8], 0.0)
                return carry

            return lax.fori_loop(0, passes, one_pass, carry)

        lax.fori_loop(0, chunks, one_chunk, 0)
        for u in range(units):
            w, side = divmod(u, LO // LANES)
            lanes = slice(side * LANES, (side + 1) * LANES)
            own_ref[:, u * LANES : (u + 1) * LANES] = acc_ref[w, bins * rows : bins * rows + 8, lanes]
            for s in range(2 * bins):
                at = s % 2 * bin_width + u * LANES
                out_ref[s // 2, :, at : at + LANES] = acc_ref[w, s * 8 : s * 8 + 8, lanes].astype(BF16)

    below = jnp.where(iota((LANES, LANES), 0) < iota((LANES, LANES), 1), 1.0, 0.0)
    below = jnp.concatenate([below, jnp.ones((LANES, LANES), F32)], axis=1).astype(BF16)
    so_far = jnp.zeros((8, LANES), F32)
    row = iota((8, LANES), 0)
    for u in range(units):
        lanes = slice(u * LANES, (u + 1) * LANES)
        odds = own_ref[:, lanes]
        count = dot(odds.astype(BF16), below)
        place_odd = so_far + count[:, :LANES]
        place_even = (iota((8, LANES), 1) + u * LANES).astype(F32) - place_odd
        so_far = so_far + count[:, LANES:]
        own_ref[:, lanes] = jnp.where(
            row == 0, jnp.where(odds == 0.0, place_even, -1.0), jnp.where(odds == 1.0, place_odd, -1.0)
        )


def partition(slot, code, start, x):
    rows, width = x.shape
    chunks, bins = start.shape[0] - 1, start.shape[1]
    bin_width = width // bins
    windows = -(-bin_width // LO)
    chunk = width // chunks
    outs = [
        jax.ShapeDtypeStruct((bins, rows // 2, 2 * bin_width + LANES), BF16),
        jax.ShapeDtypeStruct((8, bin_width), F32),
        jax.ShapeDtypeStruct((chunks, LO, chunk), BF16),
    ]
    scratch = [
        pltpu.VMEM((chunks, (bins + 1) * rows, chunk), BF16),
        pltpu.VMEM((windows, (bins + 1) * rows, LO), F32),
    ]
    inputs = [code, start, x]
    return on_core(partition_kernel, "partition", outs, [slot], inputs, 38, scratch)


def passes(a, b):
    return dot(a[0], b[0]) + (dot(a[0], b[1]) + dot(a[1], b[0]))


def product(a, b):
    half = CMAX // 2
    top = passes([x[:half] for x in a], b)
    corner = passes([x[half:] for x in a], [x[:, half:] for x in b])
    bottom = jnp.concatenate([jnp.transpose(top[:, half:]), corner], axis=1)
    return jnp.concatenate([top, bottom], axis=0)


def whole(value, reduce):
    return reduce(reduce(value, axis=0, keepdims=True), axis=1, keepdims=True)


def compaction(places_ref, parity):
    place = places_ref[pl.ds(parity, 1), :].astype(jnp.int32)
    return jnp.where(iota((CMAX, places_ref.shape[1]), 0) == place, 1.0, 0.0).astype(BF16)


def groups_of_rows(ref, bin_width):
    for at in (0, bin_width):
        block = ref[:, :, at : at + bin_width]
        yield block.reshape(block.shape[0] * block.shape[1], bin_width)


def energy_of(ref, bin_width):
    return jnp.sum(ref[:, :, 2 * bin_width :].astype(F32), axis=0)


def gram_own_kernel(slot_ref, places_ref, rows_ref, gram_ref, x_ref, energy_ref):
    bin_width = places_ref.shape[1]
    pick = compaction(places_ref, slot_ref[0] % 2)
    at = 0
    for block in groups_of_rows(rows_ref, bin_width):
        x_ref[at : at + block.shape[0], :] = dot(block, pick, ((1,), (1,))).astype(BF16)
        at += block.shape[0]
    x = x_ref[...]
    gram_ref[...] = dot(x, x, ((0,), (0,)))
    energy_ref[...] = energy_of(rows_ref, bin_width)


def gram_other_kernel(slot_ref, places_ref, rows_ref, before_ref, energy_before_ref, gram_ref, energy_ref):
    bin_width = places_ref.shape[1]
    pick = compaction(places_ref, slot_ref[0] % 2)
    blocks = [dot(block, pick, ((1,), (1,))).astype(BF16) for block in groups_of_rows(rows_ref, bin_width)]
    x = jnp.concatenate(blocks, axis=0)
    gram_ref[...] = before_ref[...] + dot(x, x, ((0,), (0,)))
    energy_ref[...] = energy_before_ref[...] + energy_of(rows_ref, bin_width)


def first_powers_kernel(gram_ref, low_ref, fourth_ref, sums_ref, *, row_count):
    covariance = gram_ref[...] * (1.0 / row_count)
    diagonal = iota((CMAX, CMAX), 0) == iota((CMAX, CMAX), 1)
    trace = whole(jnp.where(diagonal, covariance, 0.0), jnp.sum)
    shrunk = (1.0 - shrink) * covariance
    bound = whole(jnp.sum(jnp.abs(shrunk), axis=0, keepdims=True), jnp.max)
    base = jnp.where(diagonal, 1.0, 0.0) - shrunk * (1.0 / jnp.maximum(bound, 1e-30))
    row = iota((8, LANES), 0)
    sums_ref[...] = jnp.where(row == 0, trace, bound)
    parts = halves(base)
    square = product(parts, parts)
    squares = halves(square)
    low_ref[0] = base
    low_ref[1] = square
    low_ref[2] = product(squares, parts)
    fourth_ref[...] = product(squares, squares)


def eighth_power_kernel(fourth_ref, energy_ref, neighbour_ref, eighth_ref, sum_ref):
    parts = halves(fourth_ref[...])
    eighth_ref[...] = product(parts, parts)
    sum_ref[...] = energy_ref[...] + neighbour_ref[...]


def last_powers_kernel(fourth_ref, eighth_ref, twelfth_ref, last_ref):
    parts = halves(eighth_ref[...])
    twelfth_ref[...] = product(parts, halves(fourth_ref[...]))
    top, rest = halves(product(parts, parts))
    last_ref[0] = top
    last_ref[1] = rest


def inverse_kernel(
    slot_ref, sizes_ref, e0_ref, e1_ref, sums_ref, low_ref, fourth_ref, eighth_ref, twelfth_ref, last_ref, out_ref, *, entries
):
    size = sizes_ref[slot_ref[0]]
    energy = e0_ref[...] + e1_ref[...]
    average = (energy[0:1, :1] + energy[1:2, :1] + energy[2:3, :1]) * (1.0 / entries)
    trace, bound = sums_ref[0:1, :1], sums_ref[1:2, :1]
    lift = shrink * (trace / jnp.full((1, 1), size.astype(F32))) + ridge * average
    scale = 1.0 / (bound + lift)
    theta = bound * scale
    diagonal = jnp.where(iota((CMAX, CMAX), 0) == iota((CMAX, CMAX), 1), 1.0, 0.0)
    t2 = theta * theta
    t4 = t2 * t2
    t8 = t4 * t4
    low = diagonal + theta * low_ref[0] + t2 * low_ref[1] + (theta * t2) * low_ref[2]
    high = diagonal + t4 * fourth_ref[...] + t8 * eighth_ref[...] + (t4 * t8) * twelfth_ref[...]
    total = product(halves(low), halves(high))
    total = total + (t8 * t8) * product(halves(total), (last_ref[0], last_ref[1]))
    out_ref[...] = (total * scale).astype(BF16)


def whiten_own_kernel(slot_ref, places_ref, rows_ref, x_ref, inverse_ref, done_ref, next_ref):
    parity = slot_ref[0] % 2
    bin_width = places_ref.shape[1]
    mapped = dot(x_ref[...], inverse_ref[...]).astype(BF16)
    done_ref[...] = dot(mapped, compaction(places_ref, parity)).astype(BF16)
    pick = compaction(places_ref, 1 - parity)
    at = 0
    for block in groups_of_rows(rows_ref, bin_width):
        next_ref[at : at + block.shape[0], :] = dot(block, pick, ((1,), (1,))).astype(BF16)
        at += block.shape[0]


def whiten_other_kernel(slot_ref, places_ref, done_ref, x_ref, inverse_ref, out_ref):
    pick = compaction(places_ref, 1 - slot_ref[0] % 2)
    mapped = dot(x_ref[...], inverse_ref[...]).astype(BF16)
    value = (done_ref[...].astype(F32) + dot(mapped, pick)).astype(BF16)
    count, bin_width = value.shape[0] // 2, value.shape[1]
    for half in range(2):
        block = value[half * count : (half + 1) * count].reshape(out_ref.shape[0], out_ref.shape[1], bin_width)
        out_ref[:, :, half * bin_width : (half + 1) * bin_width] = block


def on_core(kernel, name, outs, scalars, arrays, mebibytes, scratch=(), work=None):
    def spec(shape):
        return pl.BlockSpec(shape, lambda i: (0,) * len(shape))

    return pl.pallas_call(
        kernel,
        grid=(1,),
        in_specs=[pl.BlockSpec(memory_space=pltpu.SMEM) for _ in scalars] + [spec(a.shape) for a in arrays],
        out_specs=[spec(out.shape) for out in outs],
        out_shape=outs,
        scratch_shapes=list(scratch),
        compiler_params=pltpu.CompilerParams(vmem_limit_bytes=mebibytes << 20),
        cost_estimate=work and pl.CostEstimate(flops=work, bytes_accessed=1 << 17, transcendentals=0),
        name=name,
    )(*scalars, *arrays)


def restore_kernel(code_ref, start_ref, hot_ref, bins_ref, out_ref, mat_ref, lhs_ref):
    bins, half_rows, bin_width = bins_ref.shape
    bin_width = bin_width // 2
    rows, width = out_ref.shape
    slots = 2 * bins
    chunks = start_ref.shape[0] - 1
    chunk = width // chunks
    units = bin_width // LANES
    windows = mat_ref.shape[0]

    for w in range(windows):
        for side in range(LO // LANES):
            u = w * (LO // LANES) + side
            lanes = slice(side * LANES, (side + 1) * LANES)
            for s in range(slots):
                if u < units:
                    at = s % 2 * bin_width + u * LANES
                    piece = bins_ref[s // 2, :, at : at + LANES].astype(F32)
                else:
                    piece = jnp.zeros((half_rows, LANES), F32)
                mat_ref[w, s * half_rows : (s + 1) * half_rows, lanes] = piece
    code = code_ref[...]
    bin_row = code >> (PLACE_BITS + 1)
    longest = longest_run(start_ref)

    def runs(c, shift, ref):
        for p in range(bins):
            window = window_of(start_ref[c, p : p + 1, :] + shift)
            pieces = []
            for r in range(p * rows, (p + 1) * rows, 8):
                value = mat_ref[0, r : r + 8]
                for w in range(1, windows):
                    value = jnp.where(window == w, mat_ref[w, r : r + 8], value)
                pieces.append(value)
            ref[p * rows : (p + 1) * rows] = jnp.concatenate(pieces, axis=0).astype(BF16)

    def choose(lhs, hot, lanes, bin_now, old):
        got = dot(lhs, hot)
        bin_rows = jnp.broadcast_to(bin_now, (8, PIECE))
        for s in range(0, rows, 8):
            value = got[s : s + 8] if old is None else old[s : s + 8]
            for p in range(1 if old is None else 0, bins):
                value = jnp.where(bin_rows == p, got[p * rows + s : p * rows + s + 8], value)
            out_ref[s : s + 8, lanes] = value.astype(BF16)

    for c in range(chunks):
        runs(c, 0.0, lhs_ref.at[c])
        lhs = lhs_ref[c]
        for at in range(0, chunk, PIECE):
            lanes = slice(c * chunk + at, c * chunk + at + PIECE)
            choose(lhs, hot_ref[c, :, at : at + PIECE], lanes, bin_row[:, lanes], None)

    @pl.when(longest > LO)
    def _():
        passes = longest.astype(jnp.int32) // LO + 1

        def one_chunk(c, carry):
            def one_pass(k, carry):
                runs(c, (k * LO).astype(F32), lhs_ref.at[0])

                def one_piece(i, carry):
                    lanes = pl.ds(pl.multiple_of(c * chunk + i * PIECE, PIECE), PIECE)
                    part = code_ref[:, lanes]
                    now = part >> (PLACE_BITS + 1)
                    turn = ((part & (2**PLACE_BITS - 1)) - bin_starts(start_ref[c], now)) >> LO_BITS
                    hot = hot_ref[c, :, pl.ds(pl.multiple_of(i * PIECE, PIECE), PIECE)]
                    choose(lhs_ref[0], hot, lanes, jnp.where(turn == k, now, -1), out_ref[:, lanes].astype(F32))
                    return carry

                return lax.fori_loop(0, chunk // PIECE, one_piece, carry)

            return lax.fori_loop(0, passes, one_pass, carry)

        lax.fori_loop(0, chunks, one_chunk, 0)


def restore(code, start, hot, bins):
    slots, half_rows, bin_width = 2 * bins.shape[0], bins.shape[1], bins.shape[2] // 2
    width = code.shape[1]
    chunks = start.shape[0] - 1
    windows = -(-bin_width // LO)
    scratch = [
        pltpu.VMEM((windows, slots * half_rows, LO), F32),
        pltpu.VMEM((chunks, slots * half_rows, LO), BF16),
    ]
    outs = [jax.ShapeDtypeStruct((2 * half_rows, width), BF16)]
    return on_core(restore_kernel, "restore", outs, [], [code, start, hot, bins], 28, scratch)[0]


def partner(x):
    return lax.ppermute(x, "samples_2", [(0, 1), (1, 0)])


def across(x, apart):
    return lax.ppermute(x, "groups", [(i, i ^ apart) for i in range(lax.axis_size("groups"))])


def exchange(x):
    return lax.all_to_all(x, CHIPS, split_axis=0, concat_axis=0, tiled=True)


def body(observed, labels, comp_sizes):
    row_local, width_local = observed.shape
    comps = comp_sizes.shape[0]
    groups = lax.axis_size("groups")
    row_count = row_local * lax.axis_size(SAMPLES)
    bin_width = 2 * width_local // comps
    slot = lax.axis_index(SAMPLES).astype(jnp.int32).reshape(1)
    code, start = places_of(comps, labels)
    message, places, hot = partition(slot, code, start, observed)
    rows = exchange(message)
    square = jax.ShapeDtypeStruct((CMAX, CMAX), F32)
    powers = jax.ShapeDtypeStruct((3, CMAX, CMAX), F32)
    narrow = jax.ShapeDtypeStruct((CMAX, CMAX), BF16)
    pair = jax.ShapeDtypeStruct((2, CMAX, CMAX), BF16)
    tall = jax.ShapeDtypeStruct((row_count // 2, CMAX), BF16)
    flat = jax.ShapeDtypeStruct((row_count // 2, bin_width), BF16)
    small = jax.ShapeDtypeStruct((8, LANES), F32)
    back = jax.ShapeDtypeStruct((rows.shape[0], rows.shape[1], 2 * bin_width), BF16)
    others = partner(rows)
    gram, x, energy = on_core(gram_own_kernel, "gram_own", [square, tall, small], [slot], [places, rows], 12)
    gram, energy = on_core(
        gram_other_kernel, "gram_other", [square, small], [slot], [places, others, gram, energy], 12
    )
    neighbour = across(energy, 1)
    build = functools.partial(first_powers_kernel, row_count=row_count)
    low, fourth, sums = on_core(build, "first_powers", [powers, square, small], [], [gram], 16)
    eighth, energy = on_core(
        eighth_power_kernel, "eighth_power", [square, small], [], [fourth, energy, neighbour], 12
    )
    others = across(energy, 2)
    twelfth, last = on_core(last_powers_kernel, "last_powers", [square, pair], [], [fourth, eighth], 16)
    finish = functools.partial(inverse_kernel, entries=row_count * width_local * groups)
    (own,) = on_core(
        finish,
        "inverse",
        [narrow],
        [slot, comp_sizes],
        [energy, others, sums, low, fourth, eighth, twelfth, last],
        24,
    )
    other = partner(own)
    done, waiting = on_core(whiten_own_kernel, "whiten_own", [flat, tall], [slot], [places, rows, x, own], 16)
    (mapped,) = on_core(
        whiten_other_kernel, "whiten_other", [back], [slot], [places, done, waiting, other], 16
    )
    return restore(code, start, hot, exchange(mapped))


def solution(mesh):
    finer = Mesh(
        mesh.devices.reshape(8, 4, 2, mesh.shape["groups"]),
        ("samples_0", "samples_1", "samples_2", "groups"),
    )
    in_specs = (P(SAMPLES, "groups"), P("groups"), P("groups"))
    out_specs = P(SAMPLES, "groups")
    return jax.shard_map(body, mesh=finer, in_specs=in_specs, out_specs=out_specs, check_vma=False)
```

```python
import functools

import jax
import jax.numpy as jnp
from jax import lax
from jax.experimental import pallas as pl
from jax.experimental.pallas import tpu as pltpu
from jax.sharding import Mesh
from jax.sharding import PartitionSpec as P

CMAX = 512
ITERS = 5
LO = 256
LO_BITS = 8
PLACE_BITS = 10
LANES = 128
CHUNKS = 4
PIECE = 1024
CHIPS = ("samples_0", "samples_1")
SAMPLES = ("samples_0", "samples_1", "samples_2")
BF16 = jnp.bfloat16
F32 = jnp.float32

shrink = 0.2
ridge = 0.5


def iota(shape, axis):
    return lax.broadcasted_iota(jnp.int32, shape, axis)


def dot(a, b, contract=((1,), (0,))):
    return lax.dot_general(a, b, (contract, ((), ())), preferred_element_type=F32)


def halves(x):
    top = x.astype(BF16)
    return top, (x - top.astype(F32)).astype(BF16)


def one_hot_lo(place, ref):
    low = jnp.broadcast_to((place & (LO - 1)).astype(F32), (16, place.shape[1])).astype(BF16)
    level = iota((LO, LANES), 0).astype(F32).astype(BF16)
    for at in range(0, place.shape[1], LANES):
        lanes = slice(at, at + LANES)
        for r in range(0, LO, 16):
            same = level[r : r + 16] == low[:, lanes]
            ref[r : r + 16, lanes] = jnp.where(same, jnp.ones((16, LANES), BF16), jnp.zeros((16, LANES), BF16))


def window_of(begin):
    begin = jnp.concatenate([begin.astype(jnp.int32)] * (LO // LANES), axis=1)
    begin = jnp.broadcast_to(begin, (8, LO))
    return (begin >> LO_BITS) + jnp.where(iota((8, LO), 1) < (begin & (LO - 1)), 1, 0)


def bin_starts(start, bin_row):
    bins = start.shape[0]
    parts = []
    for at in range(0, bin_row.shape[1], LANES):
        same = iota((bins, LANES), 0) == bin_row[:, at : at + LANES]
        parts.append(jnp.sum(jnp.where(same, start, 0.0), axis=0, keepdims=True))
    return jnp.concatenate(parts, axis=1).astype(jnp.int32)


def places_kernel(labels_ref, code_ref, start_ref):
    width = labels_ref.shape[1]
    chunks, bins = start_ref.shape[0] - 1, start_ref.shape[1]
    chunk = width // chunks
    label = labels_ref[...] & (2 * bins - 1)
    bin_row = label >> 1
    upper = jnp.where(iota((LO, LO), 0) < iota((LO, LO), 1), 1.0, 0.0)
    counting = jnp.concatenate([upper, jnp.ones((LO, LANES), F32)], axis=1).astype(BF16)
    hots = [iota((bins, LO), 0) == bin_row[:, t : t + LO] for t in range(0, width, LO)]
    ones = jnp.concatenate([jnp.where(hot, 1.0, 0.0).astype(BF16) for hot in hots], axis=0)
    counts = dot(ones, counting)
    done = jnp.zeros((bins, LANES), F32)
    places = []
    for t, hot in enumerate(hots):
        if t * LO % chunk == 0:
            start_ref[t * LO // chunk] = done
        count = counts[t * bins : (t + 1) * bins]
        inside = jnp.concatenate([done] * (LO // LANES), axis=1) + count[:, :LO]
        places.append(jnp.sum(jnp.where(hot, inside, 0.0), axis=0, keepdims=True))
        done = done + count[:, LO:]
    start_ref[chunks] = done
    place = jnp.concatenate(places, axis=1).astype(jnp.int32)
    code_ref[...] = (label << PLACE_BITS) + place


def places_of(comps, labels, chunks=CHUNKS):
    width = labels.shape[0]
    outs = [
        jax.ShapeDtypeStruct((1, width), jnp.int32),
        jax.ShapeDtypeStruct((chunks + 1, comps // 2, LANES), F32),
    ]
    return on_core(places_kernel, "places", outs, [], [labels.reshape(1, width)], 16, work=8 * 10**9)


def longest_run(start_ref):
    most = start_ref[1] - start_ref[0]
    for c in range(1, start_ref.shape[0] - 1):
        most = jnp.maximum(most, start_ref[c + 1] - start_ref[c])
    return jnp.max(most)


def partition_kernel(slot_ref, code_ref, start_ref, x_ref, out_ref, own_ref, hot_ref, lhs_ref, acc_ref):
    rows, width = x_ref.shape
    chunks, bins = start_ref.shape[0] - 1, start_ref.shape[1]
    chunk = width // chunks
    windows = acc_ref.shape[0]
    bin_width = own_ref.shape[1]
    units = bin_width // LANES
    pair = slot_ref[0] // 2
    bin_row = code_ref[...] >> (PLACE_BITS + 1)
    place = code_ref[...] & (2**PLACE_BITS - 1)
    longest = longest_run(start_ref)

    def masked(c, bin_now, ref):
        columns = slice(c * chunk, (c + 1) * chunk)
        if not isinstance(c, int):
            columns = pl.ds(pl.multiple_of(c * chunk, chunk), chunk)
        x = x_ref[:, columns]
        bin_rows = jnp.broadcast_to(bin_now.astype(F32), (rows, chunk)).astype(BF16)
        for p in range(bins):
            ref[p * rows : (p + 1) * rows, :] = jnp.where(
                bin_rows == jnp.asarray(p, BF16), x, jnp.zeros_like(x)
            )
        mine = jnp.where(bin_now == pair, (code_ref[:, columns] >> PLACE_BITS) & 1, 0).astype(F32)
        ref[bins * rows :, :] = jnp.broadcast_to(mine, (rows, chunk)).astype(BF16)

    def first_places(c, p):
        if p < bins:
            return start_ref[c, p : p + 1, :]
        return start_ref[c, pl.ds(pair, 1), :]

    runs = []
    for c in range(chunks):
        columns = slice(c * chunk, (c + 1) * chunk)
        one_hot_lo(place[:, columns], hot_ref.at[c])
        masked(c, bin_row[:, columns], lhs_ref.at[c])
        runs.append(dot(lhs_ref[c], hot_ref[c], ((1,), (1,))))

    sums = [jnp.zeros((rows, LANES), F32)] * 8
    for at in range(0, width, LANES):
        wide = x_ref[:, at : at + LANES].astype(F32)
        turn = at // LANES % len(sums)
        sums[turn] = sums[turn] + wide * wide
    while len(sums) > 1:
        sums = [a + b for a, b in zip(sums[::2], sums[1::2])]
    total = whole(sums[0], jnp.sum)
    first = total.astype(BF16).astype(F32)
    second = (total - first).astype(BF16).astype(F32)
    third = total - first - second
    row = iota((8, LANES), 0)
    pieces = jnp.where(row == 0, first, jnp.where(row == 1, second, jnp.where(row == 2, third, 0.0)))
    pieces = pieces.astype(BF16)

    for p in range(bins + 1):
        reached = [window_of(first_places(c, p)) for c in range(chunks)]
        for w in range(windows):
            hits = [window == w for window in reached]
            for half in range(2 if p < bins else 1):
                r = p * rows + half * 8
                value = jnp.where(hits[0], runs[0][r : r + 8], 0.0)
                for hit, run in zip(hits[1:], runs[1:]):
                    value = jnp.where(hit, run[r : r + 8], value)
                for side in range(LO // LANES):
                    u = w * (LO // LANES) + side
                    if u >= units:
                        continue
                    piece = value[:, side * LANES : (side + 1) * LANES]
                    if p < bins:
                        at = half * bin_width + u * LANES
                        out_ref[p, :, at : at + LANES] = piece.astype(BF16)
                    else:
                        own_ref[:, u * LANES : (u + 1) * LANES] = piece
    for p in range(bins):
        out_ref[p, :, 2 * bin_width :] = pieces

    @pl.when(longest > LO)
    def _():
        acc_ref[...] = jnp.zeros_like(acc_ref)
        passes = longest.astype(jnp.int32) // LO + 1

        def one_chunk(c, carry):
            code = code_ref[:, pl.ds(pl.multiple_of(c * chunk, chunk), chunk)]
            now = code >> (PLACE_BITS + 1)
            code = code & (2**PLACE_BITS - 1)
            turn = (code - bin_starts(start_ref[c], now)) >> LO_BITS

            def one_pass(k, carry):
                masked(c, jnp.where(turn == k, now, -1), lhs_ref.at[0])
                got = dot(lhs_ref[0], hot_ref[c], ((1,), (1,)))
                for p in range(bins + 1):
                    window = window_of(first_places(c, p) + (k * LO).astype(F32))
                    for w in range(windows):
                        for r in range(p * rows, (p + 1) * rows, 8):
                            acc_ref[w, r : r + 8] += jnp.where(window == w, got[r : r + 8], 0.0)
                return carry

            return lax.fori_loop(0, passes, one_pass, carry)

        lax.fori_loop(0, chunks, one_chunk, 0)
        for u in range(units):
            w, side = divmod(u, LO // LANES)
            lanes = slice(side * LANES, (side + 1) * LANES)
            own_ref[:, u * LANES : (u + 1) * LANES] = acc_ref[w, bins * rows : bins * rows + 8, lanes]
            for s in range(2 * bins):
                at = s % 2 * bin_width + u * LANES
                out_ref[s // 2, :, at : at + LANES] = acc_ref[w, s * 8 : s * 8 + 8, lanes].astype(BF16)

    below = jnp.where(iota((LANES, LANES), 0) < iota((LANES, LANES), 1), 1.0, 0.0)
    below = jnp.concatenate([below, jnp.ones((LANES, LANES), F32)], axis=1).astype(BF16)
    so_far = jnp.zeros((8, LANES), F32)
    row = iota((8, LANES), 0)
    for u in range(units):
        lanes = slice(u * LANES, (u + 1) * LANES)
        odds = own_ref[:, lanes]
        count = dot(odds.astype(BF16), below)
        place_odd = so_far + count[:, :LANES]
        place_even = (iota((8, LANES), 1) + u * LANES).astype(F32) - place_odd
        so_far = so_far + count[:, LANES:]
        own_ref[:, lanes] = jnp.where(
            row == 0, jnp.where(odds == 0.0, place_even, -1.0), jnp.where(odds == 1.0, place_odd, -1.0)
        )


def partition(slot, code, start, x):
    rows, width = x.shape
    chunks, bins = start.shape[0] - 1, start.shape[1]
    bin_width = width // bins
    windows = -(-bin_width // LO)
    chunk = width // chunks
    outs = [
        jax.ShapeDtypeStruct((bins, rows // 2, 2 * bin_width + LANES), BF16),
        jax.ShapeDtypeStruct((8, bin_width), F32),
        jax.ShapeDtypeStruct((chunks, LO, chunk), BF16),
    ]
    scratch = [
        pltpu.VMEM((chunks, (bins + 1) * rows, chunk), BF16),
        pltpu.VMEM((windows, (bins + 1) * rows, LO), F32),
    ]
    inputs = [code, start, x]
    return on_core(partition_kernel, "partition", outs, [slot], inputs, 38, scratch)


def passes(a, b):
    return dot(a[0], b[0]) + (dot(a[0], b[1]) + dot(a[1], b[0]))


def product(a, b):
    half = CMAX // 2
    top = passes([x[:half] for x in a], b)
    corner = passes([x[half:] for x in a], [x[:, half:] for x in b])
    bottom = jnp.concatenate([jnp.transpose(top[:, half:]), corner], axis=1)
    return jnp.concatenate([top, bottom], axis=0)


def whole(value, reduce):
    return reduce(reduce(value, axis=0, keepdims=True), axis=1, keepdims=True)


def compaction(places_ref, parity):
    place = places_ref[pl.ds(parity, 1), :].astype(jnp.int32)
    return jnp.where(iota((CMAX, places_ref.shape[1]), 0) == place, 1.0, 0.0).astype(BF16)


def groups_of_rows(ref, bin_width):
    for at in (0, bin_width):
        block = ref[:, :, at : at + bin_width]
        yield block.reshape(block.shape[0] * block.shape[1], bin_width)


def energy_of(ref, bin_width):
    return jnp.sum(ref[:, :, 2 * bin_width :].astype(F32), axis=0)


def gram_own_kernel(slot_ref, places_ref, rows_ref, gram_ref, x_ref, energy_ref):
    bin_width = places_ref.shape[1]
    pick = compaction(places_ref, slot_ref[0] % 2)
    at = 0
    for block in groups_of_rows(rows_ref, bin_width):
        x_ref[at : at + block.shape[0], :] = dot(block, pick, ((1,), (1,))).astype(BF16)
        at += block.shape[0]
    x = x_ref[...]
    gram_ref[...] = dot(x, x, ((0,), (0,)))
    energy_ref[...] = energy_of(rows_ref, bin_width)


def gram_other_kernel(slot_ref, places_ref, rows_ref, before_ref, energy_before_ref, gram_ref, energy_ref):
    bin_width = places_ref.shape[1]
    pick = compaction(places_ref, slot_ref[0] % 2)
    blocks = [dot(block, pick, ((1,), (1,))).astype(BF16) for block in groups_of_rows(rows_ref, bin_width)]
    x = jnp.concatenate(blocks, axis=0)
    gram_ref[...] = before_ref[...] + dot(x, x, ((0,), (0,)))
    energy_ref[...] = energy_before_ref[...] + energy_of(rows_ref, bin_width)


def first_powers_kernel(gram_ref, low_ref, fourth_ref, sums_ref, *, row_count):
    covariance = gram_ref[...] * (1.0 / row_count)
    diagonal = iota((CMAX, CMAX), 0) == iota((CMAX, CMAX), 1)
    trace = whole(jnp.where(diagonal, covariance, 0.0), jnp.sum)
    shrunk = (1.0 - shrink) * covariance
    bound = whole(jnp.sum(jnp.abs(shrunk), axis=0, keepdims=True), jnp.max)
    base = jnp.where(diagonal, 1.0, 0.0) - shrunk * (1.0 / jnp.maximum(bound, 1e-30))
    row = iota((8, LANES), 0)
    sums_ref[...] = jnp.where(row == 0, trace, bound)
    parts = halves(base)
    square = product(parts, parts)
    squares = halves(square)
    low_ref[0] = base
    low_ref[1] = square
    low_ref[2] = product(squares, parts)
    fourth_ref[...] = product(squares, squares)


def eighth_power_kernel(fourth_ref, energy_ref, neighbour_ref, eighth_ref, sum_ref):
    parts = halves(fourth_ref[...])
    eighth_ref[...] = product(parts, parts)
    sum_ref[...] = energy_ref[...] + neighbour_ref[...]


def last_powers_kernel(fourth_ref, eighth_ref, twelfth_ref, last_ref):
    parts = halves(eighth_ref[...])
    twelfth_ref[...] = product(parts, halves(fourth_ref[...]))
    top, rest = halves(product(parts, parts))
    last_ref[0] = top
    last_ref[1] = rest


def inverse_kernel(
    slot_ref, sizes_ref, e0_ref, e1_ref, sums_ref, low_ref, fourth_ref, eighth_ref, twelfth_ref, last_ref, out_ref, *, entries
):
    size = sizes_ref[slot_ref[0]]
    energy = e0_ref[...] + e1_ref[...]
    average = (energy[0:1, :1] + energy[1:2, :1] + energy[2:3, :1]) * (1.0 / entries)
    trace, bound = sums_ref[0:1, :1], sums_ref[1:2, :1]
    lift = shrink * (trace / jnp.full((1, 1), size.astype(F32))) + ridge * average
    scale = 1.0 / (bound + lift)
    theta = bound * scale
    diagonal = jnp.where(iota((CMAX, CMAX), 0) == iota((CMAX, CMAX), 1), 1.0, 0.0)
    t2 = theta * theta
    t4 = t2 * t2
    t8 = t4 * t4
    low = diagonal + theta * low_ref[0] + t2 * low_ref[1] + (theta * t2) * low_ref[2]
    high = diagonal + t4 * fourth_ref[...] + t8 * eighth_ref[...] + (t4 * t8) * twelfth_ref[...]
    total = product(halves(low), halves(high))
    total = total + (t8 * t8) * product(halves(total), (last_ref[0], last_ref[1]))
    out_ref[...] = (total * scale).astype(BF16)


def whiten_own_kernel(slot_ref, places_ref, rows_ref, x_ref, inverse_ref, done_ref, next_ref):
    parity = slot_ref[0] % 2
    bin_width = places_ref.shape[1]
    mapped = dot(x_ref[...], inverse_ref[...]).astype(BF16)
    done_ref[...] = dot(mapped, compaction(places_ref, parity)).astype(BF16)
    pick = compaction(places_ref, 1 - parity)
    at = 0
    for block in groups_of_rows(rows_ref, bin_width):
        next_ref[at : at + block.shape[0], :] = dot(block, pick, ((1,), (1,))).astype(BF16)
        at += block.shape[0]


def whiten_other_kernel(slot_ref, places_ref, done_ref, x_ref, inverse_ref, out_ref):
    pick = compaction(places_ref, 1 - slot_ref[0] % 2)
    mapped = dot(x_ref[...], inverse_ref[...]).astype(BF16)
    value = (done_ref[...].astype(F32) + dot(mapped, pick)).astype(BF16)
    count, bin_width = value.shape[0] // 2, value.shape[1]
    for half in range(2):
        block = value[half * count : (half + 1) * count].reshape(out_ref.shape[0], out_ref.shape[1], bin_width)
        out_ref[:, :, half * bin_width : (half + 1) * bin_width] = block


def on_core(kernel, name, outs, scalars, arrays, mebibytes, scratch=(), work=None):
    def spec(shape):
        return pl.BlockSpec(shape, lambda i: (0,) * len(shape))

    return pl.pallas_call(
        kernel,
        grid=(1,),
        in_specs=[pl.BlockSpec(memory_space=pltpu.SMEM) for _ in scalars] + [spec(a.shape) for a in arrays],
        out_specs=[spec(out.shape) for out in outs],
        out_shape=outs,
        scratch_shapes=list(scratch),
        compiler_params=pltpu.CompilerParams(vmem_limit_bytes=mebibytes << 20),
        cost_estimate=work and pl.CostEstimate(flops=work, bytes_accessed=1 << 17, transcendentals=0),
        name=name,
    )(*scalars, *arrays)


def restore_kernel(code_ref, start_ref, hot_ref, bins_ref, out_ref, mat_ref, lhs_ref):
    bins, half_rows, bin_width = bins_ref.shape
    bin_width = bin_width // 2
    rows, width = out_ref.shape
    slots = 2 * bins
    chunks = start_ref.shape[0] - 1
    chunk = width // chunks
    units = bin_width // LANES
    windows = mat_ref.shape[0]

    for w in range(windows):
        for side in range(LO // LANES):
            u = w * (LO // LANES) + side
            lanes = slice(side * LANES, (side + 1) * LANES)
            for s in range(slots):
                if u < units:
                    at = s % 2 * bin_width + u * LANES
                    piece = bins_ref[s // 2, :, at : at + LANES].astype(F32)
                else:
                    piece = jnp.zeros((half_rows, LANES), F32)
                mat_ref[w, s * half_rows : (s + 1) * half_rows, lanes] = piece
    code = code_ref[...]
    bin_row = code >> (PLACE_BITS + 1)
    longest = longest_run(start_ref)

    def runs(c, shift, ref):
        for p in range(bins):
            window = window_of(start_ref[c, p : p + 1, :] + shift)
            pieces = []
            for r in range(p * rows, (p + 1) * rows, 8):
                value = mat_ref[0, r : r + 8]
                for w in range(1, windows):
                    value = jnp.where(window == w, mat_ref[w, r : r + 8], value)
                pieces.append(value)
            ref[p * rows : (p + 1) * rows] = jnp.concatenate(pieces, axis=0).astype(BF16)

    def choose(lhs, hot, lanes, bin_now, old):
        got = dot(lhs, hot)
        bin_rows = jnp.broadcast_to(bin_now, (8, PIECE))
        for s in range(0, rows, 8):
            value = got[s : s + 8] if old is None else old[s : s + 8]
            for p in range(1 if old is None else 0, bins):
                value = jnp.where(bin_rows == p, got[p * rows + s : p * rows + s + 8], value)
            out_ref[s : s + 8, lanes] = value.astype(BF16)

    for c in range(chunks):
        runs(c, 0.0, lhs_ref.at[c])
        lhs = lhs_ref[c]
        for at in range(0, chunk, PIECE):
            lanes = slice(c * chunk + at, c * chunk + at + PIECE)
            choose(lhs, hot_ref[c, :, at : at + PIECE], lanes, bin_row[:, lanes], None)

    @pl.when(longest > LO)
    def _():
        passes = longest.astype(jnp.int32) // LO + 1

        def one_chunk(c, carry):
            def one_pass(k, carry):
                runs(c, (k * LO).astype(F32), lhs_ref.at[0])

                def one_piece(i, carry):
                    lanes = pl.ds(pl.multiple_of(c * chunk + i * PIECE, PIECE), PIECE)
                    part = code_ref[:, lanes]
                    now = part >> (PLACE_BITS + 1)
                    turn = ((part & (2**PLACE_BITS - 1)) - bin_starts(start_ref[c], now)) >> LO_BITS
                    hot = hot_ref[c, :, pl.ds(pl.multiple_of(i * PIECE, PIECE), PIECE)]
                    choose(lhs_ref[0], hot, lanes, jnp.where(turn == k, now, -1), out_ref[:, lanes].astype(F32))
                    return carry

                return lax.fori_loop(0, chunk // PIECE, one_piece, carry)

            return lax.fori_loop(0, passes, one_pass, carry)

        lax.fori_loop(0, chunks, one_chunk, 0)


def restore(code, start, hot, bins):
    slots, half_rows, bin_width = 2 * bins.shape[0], bins.shape[1], bins.shape[2] // 2
    width = code.shape[1]
    chunks = start.shape[0] - 1
    windows = -(-bin_width // LO)
    scratch = [
        pltpu.VMEM((windows, slots * half_rows, LO), F32),
        pltpu.VMEM((chunks, slots * half_rows, LO), BF16),
    ]
    outs = [jax.ShapeDtypeStruct((2 * half_rows, width), BF16)]
    return on_core(restore_kernel, "restore", outs, [], [code, start, hot, bins], 28, scratch)[0]


def partner(x):
    return lax.ppermute(x, "samples_2", [(0, 1), (1, 0)])


def across(x, apart):
    return lax.ppermute(x, "groups", [(i, i ^ apart) for i in range(lax.axis_size("groups"))])


def exchange(x):
    return lax.all_to_all(x, CHIPS, split_axis=0, concat_axis=0, tiled=True)


def body(observed, labels, comp_sizes):
    row_local, width_local = observed.shape
    comps = comp_sizes.shape[0]
    groups = lax.axis_size("groups")
    row_count = row_local * lax.axis_size(SAMPLES)
    bin_width = 2 * width_local // comps
    slot = lax.axis_index(SAMPLES).astype(jnp.int32).reshape(1)
    code, start = places_of(comps, labels)
    message, places, hot = partition(slot, code, start, observed)
    rows = exchange(message)
    square = jax.ShapeDtypeStruct((CMAX, CMAX), F32)
    powers = jax.ShapeDtypeStruct((3, CMAX, CMAX), F32)
    narrow = jax.ShapeDtypeStruct((CMAX, CMAX), BF16)
    pair = jax.ShapeDtypeStruct((2, CMAX, CMAX), BF16)
    tall = jax.ShapeDtypeStruct((row_count // 2, CMAX), BF16)
    flat = jax.ShapeDtypeStruct((row_count // 2, bin_width), BF16)
    small = jax.ShapeDtypeStruct((8, LANES), F32)
    back = jax.ShapeDtypeStruct((rows.shape[0], rows.shape[1], 2 * bin_width), BF16)
    others = partner(rows)
    gram, x, energy = on_core(gram_own_kernel, "gram_own", [square, tall, small], [slot], [places, rows], 12)
    gram, energy = on_core(
        gram_other_kernel, "gram_other", [square, small], [slot], [places, others, gram, energy], 12
    )
    neighbour = across(energy, 1)
    build = functools.partial(first_powers_kernel, row_count=row_count)
    low, fourth, sums = on_core(build, "first_powers", [powers, square, small], [], [gram], 16)
    eighth, energy = on_core(
        eighth_power_kernel, "eighth_power", [square, small], [], [fourth, energy, neighbour], 12
    )
    others = across(energy, 2)
    twelfth, last = on_core(last_powers_kernel, "last_powers", [square, pair], [], [fourth, eighth], 16)
    finish = functools.partial(inverse_kernel, entries=row_count * width_local * groups)
    (own,) = on_core(
        finish,
        "inverse",
        [narrow],
        [slot, comp_sizes],
        [energy, others, sums, low, fourth, eighth, twelfth, last],
        24,
    )
    other = partner(own)
    done, waiting = on_core(whiten_own_kernel, "whiten_own", [flat, tall], [slot], [places, rows, x, own], 16)
    (mapped,) = on_core(
        whiten_other_kernel, "whiten_other", [back], [slot], [places, done, waiting, other], 16
    )
    return restore(code, start, hot, exchange(mapped))


def solution(mesh):
    finer = Mesh(
        mesh.devices.reshape(8, 4, 2, mesh.shape["groups"]),
        ("samples_0", "samples_1", "samples_2", "groups"),
    )
    in_specs = (P(SAMPLES, "groups"), P("groups"), P("groups"))
    out_specs = P(SAMPLES, "groups")
    return jax.shard_map(body, mesh=finer, in_specs=in_specs, out_specs=out_specs, check_vma=False)
```
